32 devices in a mesh: row: 4 (over y, x), col: 8 (over z, core).
Axes of the slice: x: 2, y: 2, z: 4, core: 2. Of those that a mesh axis runs over, the one named last changes fastest.
Arguments:
- cov: float32 [18432, 18432], P('row', 'col'), may hold values from -1 to 70, as said below
- weights: float32 [18432], P(('row', 'col')), may hold values from -0.6 to 0.6
- act: bfloat16 [8, 512, 144], P('row', 'col'), may hold values from -6 to 6
- upstream: bfloat16 [8, 512, 128], P('row', 'col'), may hold values from -6 to 6
- neighbors: int32 [8, 512, 138], P('row', 'col'), may hold values from 0 to 511
- types: int32 [8, 512], P('row', 'col'), may hold values from 0 to 1
- type_gain: float32 [2, 128], replicated, may hold values from 0.25 to 1.75
- sens: float32 [64, 512], P('row', 'col'), may hold values from -0.0009765625 to 0.0009765625
- frame_for_measure: int32 [64], P('row'), may hold values from 0 to 1
- noise_variance: float32 [64], replicated, may hold values from 0.5 to 2
- innovation: float32 [64], replicated, may hold values from -6 to 6
Outputs:
- weights_new: float32 [18432], P(('row', 'col'))
- cov_new: float32 [18432, 18432], P('row', 'col')
The draws below stay inside these ranges and needn't reach their ends.
Inputs may be any that keep to these rules, and one draw needn't show every extreme that they name: cov is symmetric and positive definite.
All inputs are finite; a program needn't handle non-finite values. Where the reference program divides by a largest or mean magnitude, that divisor is 1e-20 or more.
Results may differ from the reference program's by a relative error of at most 0.0023.
Values may be sent and summed in bfloat16 or wider, within the bound.
No kernel may reach another device: no remote copies, remote signals or barrier semaphores. Data moves between devices by JAX's collectives and lax.ppermute only.
A program may use at most 128 MiB of HBM per device.

```python
import math
import jax
import jax.numpy as jnp
from jax import lax

ACTW = 144
ADJW = 128
NBR = 138
NTYPES = 2
NS_ITERS = 5
FRAME_GROUP = 2
MEASURE_GROUP = 16
BLOCK_WEIGHTS = 18432
ATOM_COUNT = 512
FRAMES = 8
MEASURE_TOTAL = 64


def draw_cov(key, part):
    noise_key, diag_key, scale_key = jax.random.split(key, 3)
    raw_noise = jax.random.normal(noise_key, (BLOCK_WEIGHTS, BLOCK_WEIGHTS), jnp.float32)
    spread = jax.random.uniform(scale_key, (BLOCK_WEIGHTS,), jnp.float32, 0.0, 2.3025851)
    symmetric = (raw_noise + raw_noise.T) * (0.25 / jnp.sqrt(2.0 * BLOCK_WEIGHTS))
    lifted = 1.0 + jax.random.uniform(diag_key, (BLOCK_WEIGHTS,), jnp.float32)
    diagonal_at = jnp.arange(BLOCK_WEIGHTS, dtype=jnp.int32)
    symmetric = symmetric.at[diagonal_at, diagonal_at].add(lifted)
    scales = jnp.exp(0.5 * spread)
    return symmetric * (scales[:, None] * scales[None, :])


def plant(result, key, low, high):
    extent = result.shape
    index_at = [jax.random.randint(jax.random.fold_in(key, axis), (), 0, extent[axis]) for axis in range(len(extent))]
    result = result.at[tuple(index_at)].set(low)
    longest = extent.index(max(extent))
    index_at[longest] = (index_at[longest] + 1) % extent[longest]
    return result.at[tuple(index_at)].set(high)


def block_levels(rng, dims, cuts, low, high):
    def one(axis_at, parts):
        heights = jax.random.uniform(jax.random.fold_in(jax.random.fold_in(rng, 6), axis_at), (parts,), jnp.float32, low / len(cuts), high / len(cuts))
        return jnp.repeat(jnp.exp(heights), dims[axis_at] // parts).reshape((-1,) + (1,) * (len(dims) - axis_at - 1))

    level = one(*cuts[0])
    for cut in cuts[1:]:
        level = level * one(*cut)
    return level


def scatter_about(key, dims, deviation, most, cuts=(), kind=jnp.bfloat16):
    entries = jax.random.normal(key, dims, jnp.float32) * deviation
    if len(cuts) > 0:
        entries = block_levels(key, dims, cuts, -0.22, 0.18) * entries
    return jnp.clip(entries, min=-most, max=most).astype(kind)


def setup_inputs(seed: int = 0) -> dict:
    splits = jax.random.split(jax.random.key(seed), 12)
    cov = draw_cov(jax.random.fold_in(splits[11], 71), 0)
    weights = scatter_about(splits[1], (BLOCK_WEIGHTS,), 0.1, 0.6, ((0, 32),), jnp.float32)
    act = scatter_about(splits[2], (FRAMES, ATOM_COUNT, ACTW), 1.0, 6.0, ((0, 4), (1, 8)))
    upstream = scatter_about(splits[3], (FRAMES, ATOM_COUNT, ADJW), 1.0, 6.0, ((0, 4), (1, 8)))
    neighbors = plant(jax.random.randint(splits[4], (FRAMES, ATOM_COUNT, NBR), 0, ATOM_COUNT), jax.random.fold_in(splits[4], 1), 0, ATOM_COUNT - 1).astype(jnp.int32)
    types = plant(jax.random.randint(splits[5], (FRAMES, ATOM_COUNT), 0, NTYPES), jax.random.fold_in(splits[5], 1), 0, NTYPES - 1).astype(jnp.int32)
    type_gain = jnp.clip(1.0 + 0.15 * jax.random.normal(splits[6], (NTYPES, ADJW), jnp.float32), 0.25, 1.75)
    sens = scatter_about(splits[7], (MEASURE_TOTAL, ATOM_COUNT), (0.5 / (ATOM_COUNT * BLOCK_WEIGHTS) ** 0.5), 0.0009765625, ((0, 4), (1, 8)), jnp.float32)
    frame_for_measure = plant(jax.random.randint(splits[8], (MEASURE_TOTAL,), 0, FRAME_GROUP), jax.random.fold_in(splits[8], 1), 0, FRAME_GROUP - 1).astype(jnp.int32)
    noise_variance = jnp.clip(jnp.exp(jax.random.uniform(splits[9], (MEASURE_TOTAL,), jnp.float32, math.log(0.5), math.log(2.0))), 0.5, 2.0)
    innovation = scatter_about(splits[10], (MEASURE_TOTAL,), 1.0, 6.0, (), jnp.float32)
    return dict(cov=cov, weights=weights, act=act, upstream=upstream, neighbors=neighbors, types=types, type_gain=type_gain, sens=sens, frame_for_measure=frame_for_measure, noise_variance=noise_variance, innovation=innovation)


FULL_PRECISION = lax.Precision.HIGHEST

def frame_adjoint(pieces):
    lookup, indices, kinds, type_gain = pieces
    picked = jnp.take(lookup, indices, axis=0)
    neighbor_sum = lax.optimization_barrier(jnp.sum(picked, axis=1, dtype=jnp.float32)) * (1.0 / math.sqrt(NBR))
    type_scale = jnp.take(type_gain, kinds, axis=0)
    return type_scale * (lookup.astype(jnp.float32) + neighbor_sum)

def reference(cov, weights, act, upstream, neighbors, types, type_gain, sens, frame_for_measure, noise_variance, innovation):
    adjoint = lax.map(lambda pieces: frame_adjoint((pieces[0], pieces[1], pieces[2], type_gain)), (upstream, neighbors, types))
    frame_numbers = FRAME_GROUP * (jnp.arange(MEASURE_TOTAL, dtype=jnp.int32) // MEASURE_GROUP) + frame_for_measure.astype(jnp.int32)

    def jacobian_row(pieces):
        weight_row, frame_id = pieces
        weighted = (weight_row[:, None] * adjoint[frame_id]).astype(jnp.bfloat16)
        return jnp.dot(weighted.T, act[frame_id], preferred_element_type=jnp.float32).reshape(-1)
    jacobian = lax.map(jacobian_row, (sens, frame_numbers))
    numerator = jnp.dot(cov, jacobian.T, precision=FULL_PRECISION)
    innovation_cov = jnp.dot(jacobian, numerator, precision=FULL_PRECISION) + jnp.diag(noise_variance)
    scale_factor = 1.0 / jnp.max(lax.optimization_barrier(jnp.sum(jnp.abs(innovation_cov), axis=1)))
    inverse_matrix = jnp.eye(MEASURE_TOTAL, dtype=jnp.float32) * scale_factor
    for sweep in range(NS_ITERS):
        inverse_matrix = 2.0 * inverse_matrix - jnp.dot(jnp.dot(inverse_matrix, innovation_cov, precision=FULL_PRECISION), inverse_matrix, precision=FULL_PRECISION)
    gain = jnp.dot(numerator, inverse_matrix, precision=FULL_PRECISION)
    weights_new = weights + jnp.dot(gain, innovation, precision=FULL_PRECISION)
    cov_new = cov - jnp.dot(gain, numerator.T, precision=FULL_PRECISION)
    return (weights_new, cov_new)
```

```python
import functools
import math

import jax
import jax.numpy as jnp
from jax import lax
from jax.experimental import pallas as pl
from jax.experimental.pallas import tpu as pltpu
from jax.sharding import PartitionSpec as P

NS_ITERS = 5
FULL = lax.Precision.HIGHEST
F32 = jnp.float32
BF16 = jnp.bfloat16

VMEM = pl.BlockSpec(memory_space=pltpu.VMEM)
SMEM = pl.BlockSpec(memory_space=pltpu.SMEM)


def swap(block, axis, step):
    n = lax.axis_size(axis)
    return lax.ppermute(block, axis, [(i, i ^ step) for i in range(n)])


def gather(block, axis):
    return [block] + [swap(block, axis, k) for k in range(1, lax.axis_size(axis))]


def params(mib):
    return pltpu.CompilerParams(vmem_limit_bytes=mib * 2**20)


def shape(dims, kind=F32):
    return jax.ShapeDtypeStruct(dims, kind)


def estimate(flops, moved):
    return pl.CostEstimate(flops=flops, bytes_accessed=moved, transcendentals=0)


def counts_kernel(neighbors_ref, counts_ref, flipped):
    frames, atoms, slots = neighbors_ref.shape
    lanes = frames * atoms
    whole, _ = counts_ref.shape
    flipped[...] = neighbors_ref[...].reshape(lanes, slots).T
    chunk = min(256, whole)
    unroll = next(u for u in (6, 4, 3, 2, 1) if slots % u == 0)
    for base in range(0, whole, chunk):
        atom = lax.broadcasted_iota(jnp.int32, (chunk, lanes), 0) + base

        def step(s, total):
            for u in range(unroll):
                row = flipped[pl.ds(s * unroll + u, 1), :]
                total = jnp.where(atom == row, total + 1.0, total)
            return total

        total = lax.fori_loop(0, slots // unroll, step, jnp.zeros((chunk, lanes), F32))
        counts_ref[pl.ds(base, chunk), :] = total.astype(BF16)


def adjoint_kernel(slots, *refs):
    where_ref, frame_ref, counts_ref, types_ref, gain_ref, sens_ref = refs[:6]
    pieces, (out_ref, lookup) = refs[6:-2], refs[-2:]
    frames, atoms, width = pieces[0].shape
    lanes = frames * atoms
    me = where_ref[0]
    for k, piece in enumerate(pieces):
        start = pl.multiple_of((me ^ k) * atoms, atoms)
        for f in range(frames):
            lookup[f, pl.ds(start, atoms), :] = piece[f]
    lane = lax.broadcasted_iota(jnp.int32, (1, lanes), 1)
    total = jnp.zeros((width, lanes), F32)
    for f in range(frames):
        part = lax.dot_general(
            lookup[f], counts_ref[...], (((0,), (0,)), ((), ())), preferred_element_type=F32
        )
        total = jnp.where((lane // atoms) == f, part, total)
    own = pieces[0][...].reshape(lanes, width).astype(F32).T
    total = own + total * (1.0 / math.sqrt(slots))
    kinds = jnp.concatenate([types_ref[f : f + 1, :] for f in range(frames)], axis=1)
    gain = gain_ref[...].T
    scale = jnp.zeros((width, lanes), F32)
    for t in range(gain_ref.shape[0]):
        scale = jnp.where(kinds == t, gain[:, t : t + 1], scale)
    out_ref[pl.ds(0, width), :] = scale * total
    sens = sens_ref[...]
    measures = sens.shape[0]
    index = lax.broadcasted_iota(jnp.int32, sens.shape, 0)
    frame = jnp.zeros(sens.shape, jnp.int32)
    for m in range(measures):
        frame = jnp.where(index == m, frame_ref[m], frame)
    out_ref[pl.ds(width, measures), :] = jnp.concatenate(
        [jnp.where(frame == f, sens, 0.0) for f in range(frames)], axis=1
    )


def jacobian_kernel(count, row_peers, *refs):
    where_ref, sides, acts = refs[0], refs[1 : 1 + count], refs[1 + count : 1 + 2 * count]
    outs = refs[1 + 2 * count : -3]
    inputs, mixed, flat = refs[-3:]
    row, col = where_ref[0], where_ref[1]
    frames, atoms, width_in = acts[0].shape
    lanes = frames * atoms
    measures = outs[0].shape[0]
    width_out = sides[0].shape[0] - measures
    for k, act in enumerate(acts):
        inputs[pl.ds(k * lanes, lanes), :] = act[...].reshape(lanes, width_in)

    def block(out_ref, first):
        held = out_ref.shape[1] // width_in
        size = min(8, held)

        def group(g, carry):
            start = first + g * size
            for k, side in enumerate(sides):
                sens = side[pl.ds(width_out, measures), :]
                for b in range(size):
                    line = side[pl.ds(start + b, 1), :]
                    mixed[pl.ds(b * measures, measures), pl.ds(k * lanes, lanes)] = (
                        sens * line
                    ).astype(BF16)
            found = jnp.dot(
                mixed[pl.ds(0, size * measures), :], inputs[...], preferred_element_type=F32
            )
            for b in range(size):
                flat[:, pl.ds(b * width_in, width_in)] = found[
                    b * measures : (b + 1) * measures, :
                ]
            span = size * width_in
            at = g * span
            if span % 128 == 0:
                at = pl.multiple_of(at, 128)
            out_ref[:, pl.ds(at, span)] = flat[:, pl.ds(0, span)].astype(BF16)
            return carry

        if held == size:
            group(0, 0)
        else:
            lax.fori_loop(0, held // size, group, 0)

    for k in range(row_peers):
        block(outs[k], (row ^ k) * (outs[k].shape[1] // width_in))
    block(outs[row_peers], col * (outs[row_peers].shape[1] // width_in))


def product_kernel(peers, *refs):
    where_ref, jac_refs, side_refs = refs[0], refs[1 : 1 + peers], refs[1 + peers : 1 + 2 * peers]
    cov_ref = refs[1 + 2 * peers]
    outs = refs[2 + 2 * peers : 2 + 3 * peers]
    jac, side, total = refs[2 + 3 * peers :]
    me = where_ref[0]
    step = pl.program_id(0)
    measures = jac_refs[0].shape[0]
    depth, width = cov_ref.shape

    @pl.when(step == 0)
    def _():
        for k in range(peers):
            at = pl.multiple_of((me ^ k) * measures, measures)
            jac[pl.ds(at, measures), :] = jac_refs[k][...]
            side[pl.ds(at, measures), :] = side_refs[k][...].astype(F32)
        total[...] = jnp.zeros_like(total)

    left = jac[:, pl.ds(pl.multiple_of(step * depth, depth), depth)]
    block = cov_ref[...]
    high = block.astype(BF16)
    low = (block - high.astype(F32)).astype(BF16)
    total[...] += jnp.dot(left, high, preferred_element_type=F32) + jnp.dot(
        left, low, preferred_element_type=F32
    )

    @pl.when(step == pl.num_programs(0) - 1)
    def _():
        overall = measures * peers
        inner = lax.dot_general(
            total[...], side[...], (((1,), (1,)), ((), ())), precision=FULL, preferred_element_type=F32
        )
        for k in range(peers):
            at = pl.multiple_of((me ^ k) * measures, measures)
            outs[k][:, pl.ds(0, width)] = total[pl.ds(at, measures), :]
            for q in range(peers):
                outs[k][:, pl.ds(width + q * overall, overall)] = inner[
                    q * measures : (q + 1) * measures, :
                ]


def sum_kernel(peers, *refs):
    parts = refs[:peers]
    exact_ref, sent_ref, inner_ref = refs[peers:]
    measures, width = exact_ref.shape
    overall = inner_ref.shape[0]
    total = parts[0][...]
    for k in range(1, peers):
        total = total + parts[k][...]
    exact_ref[...] = total[:, :width]
    sent_ref[...] = total[:, :width].astype(BF16)
    for q in range(peers):
        inner_ref[pl.ds(q * measures, measures), :] = total[
            :, width + q * overall : width + (q + 1) * overall
        ]


def route_kernel(count, peers, *refs):
    where_ref, pieces, outs, held = refs[0], refs[1 : 1 + count], refs[1 + count : -1], refs[-1]
    row, col = where_ref[0], where_ref[1]
    width = pieces[0].shape[1]
    per_block = count // peers
    for k in range(count):
        held[col ^ k] = pieces[k][...]
    for k in range(peers):
        for p in range(per_block):
            outs[k][:, pl.ds(p * width, width)] = held[(row ^ k) * per_block + p]
        outs[k][:, pl.ds(per_block * width, width)] = pieces[0][...]


def inverse_kernel(count, peers, *refs):
    where_ref, inner_refs = refs[0], refs[1 : 1 + count]
    exact_ref, noise_ref, innovation_ref, inverse_ref, change_ref, weight = refs[1 + count :]
    row = where_ref[0]
    overall = inverse_ref.shape[0]
    measures, width = exact_ref.shape
    inner = inner_refs[0][...]
    for k in range(1, count):
        inner = inner + inner_refs[k][...]
    down = lax.broadcasted_iota(jnp.int32, (overall, overall), 0)
    across = lax.broadcasted_iota(jnp.int32, (overall, overall), 1)
    diagonal = down == across
    inner = inner + jnp.where(diagonal, noise_ref[...], 0.0)
    scale = 1.0 / jnp.max(jnp.sum(jnp.abs(inner), axis=1, keepdims=True), axis=0, keepdims=True)
    inverse = jnp.where(diagonal, scale, 0.0)
    for _ in range(NS_ITERS):
        left = jnp.dot(inverse, inner, precision=FULL, preferred_element_type=F32)
        inverse = 2.0 * inverse - jnp.dot(left, inverse, precision=FULL, preferred_element_type=F32)
    inverse_ref[...] = inverse
    weight[...] = jnp.sum(inverse * innovation_ref[...], axis=1, keepdims=True)
    mine = weight[pl.ds(pl.multiple_of(row * measures, measures), measures), :]
    change = jnp.sum(exact_ref[...] * mine, axis=0, keepdims=True)
    part = width // peers
    for q in range(peers):
        change_ref[row ^ q] = change[:, q * part : (q + 1) * part]


def update_kernel(peers, *refs):
    where_ref, pieces = refs[0], refs[1 : 1 + peers]
    inverse_ref, cov_ref, out_ref, left, right, staged = refs[1 + peers :]
    me = where_ref[0]
    step = pl.program_id(0)
    measures = pieces[0].shape[0]
    depth, width = cov_ref.shape
    height = left.shape[1]

    @pl.when(step == 0)
    def _():
        for k in range(peers):
            at = pl.multiple_of((me ^ k) * measures, measures)
            staged[pl.ds(at, measures), :] = pieces[k][:, pl.ds(0, height)].astype(F32)
            right[pl.ds(at, measures), :] = pieces[k][:, pl.ds(height, width)]
        left[...] = lax.dot_general(
            inverse_ref[...],
            staged[...],
            (((0,), (0,)), ((), ())),
            precision=FULL,
            preferred_element_type=F32,
        ).astype(BF16)

    gain = left[:, pl.ds(pl.multiple_of(step * depth, depth), depth)]
    out_ref[...] = cov_ref[...] - lax.dot_general(
        gain, right[...], (((0,), (0,)), ((), ())), preferred_element_type=F32
    )


def on_device(
    cov,
    weights,
    act,
    upstream,
    neighbors,
    types,
    type_gain,
    sens,
    frame_for_measure,
    noise_variance,
    innovation,
):
    rows, cols = lax.axis_size("row"), lax.axis_size("col")
    row, col = lax.axis_index("row"), lax.axis_index("col")
    place = jnp.stack([row, col]).astype(jnp.int32)
    frames, atoms, width_in = act.shape
    width_out = upstream.shape[2]
    slots = neighbors.shape[2]
    lanes = frames * atoms
    measures = sens.shape[0]
    overall = measures * rows
    height, width = cov.shape
    part = weights.shape[0]

    ups = gather(upstream, "col")
    acts = gather(act, "col")
    counts = pl.pallas_call(
        counts_kernel,
        out_shape=shape((atoms * cols, lanes), BF16),
        in_specs=[VMEM],
        out_specs=VMEM,
        scratch_shapes=[pltpu.VMEM((slots, lanes), jnp.int32)],
        compiler_params=params(16),
        cost_estimate=estimate(10**9, lanes * slots * 4),
        name="counts",
    )(neighbors)
    side = pl.pallas_call(
        functools.partial(adjoint_kernel, slots),
        out_shape=shape((width_out + measures, lanes)),
        in_specs=[SMEM, SMEM] + [VMEM] * (4 + cols),
        out_specs=VMEM,
        scratch_shapes=[pltpu.VMEM((frames, atoms * cols, width_out), BF16)],
        compiler_params=params(16),
        name="adjoint",
    )(place[1:], frame_for_measure, counts, types, type_gain, sens, *ups)
    sides = gather(side, "col")
    jacs = pl.pallas_call(
        functools.partial(jacobian_kernel, cols, rows),
        out_shape=[shape((measures, height), BF16)] * rows + [shape((measures, width), BF16)],
        in_specs=[SMEM] + [VMEM] * (2 * cols),
        out_specs=[VMEM] * (rows + 1),
        scratch_shapes=[
            pltpu.VMEM((cols * lanes, width_in), BF16),
            pltpu.VMEM((8 * measures, cols * lanes), BF16),
            pltpu.VMEM((measures, 8 * width_in), F32),
        ],
        compiler_params=params(24),
        name="jacobian",
    )(place, *sides, *acts)
    jac_rows = [jacs[0]] + [swap(jacs[k], "row", k) for k in range(1, rows)]
    jac_cols = gather(jacs[rows], "row")

    depth = next(d for d in (256, 128) if height % d == 0)
    parts = pl.pallas_call(
        functools.partial(product_kernel, rows),
        out_shape=[shape((measures, width + overall * rows))] * rows,
        grid=(height // depth,),
        in_specs=[SMEM] + [VMEM] * (2 * rows) + [pl.BlockSpec((depth, width), lambda i: (i, 0))],
        out_specs=[VMEM] * rows,
        scratch_shapes=[
            pltpu.VMEM((overall, height), BF16),
            pltpu.VMEM((overall, width), F32),
            pltpu.VMEM((overall, width), F32),
        ],
        compiler_params=params(40),
        cost_estimate=estimate(4 * overall * height * width, 4 * height * width),
        name="product",
    )(place[:1], *jac_rows, *jac_cols, cov)
    parts = [parts[0]] + [swap(parts[k], "row", k) for k in range(1, rows)]
    exact, sent, inner = pl.pallas_call(
        functools.partial(sum_kernel, rows),
        out_shape=[
            shape((measures, width)),
            shape((measures, width), BF16),
            shape((overall, overall)),
        ],
        in_specs=[VMEM] * rows,
        out_specs=[VMEM] * 3,
        compiler_params=params(16),
        name="sum",
    )(*parts)
    inners = gather(inner, "col")
    sents = gather(sent, "col")
    routed = pl.pallas_call(
        functools.partial(route_kernel, cols, rows),
        out_shape=[shape((measures, height + width), BF16)] * rows,
        in_specs=[SMEM] + [VMEM] * cols,
        out_specs=[VMEM] * rows,
        scratch_shapes=[pltpu.VMEM((cols, measures, width), BF16)],
        compiler_params=params(16),
        name="route",
    )(place, *sents)
    routed = [routed[0]] + [swap(routed[k], "row", k) for k in range(1, rows)]
    inverse, change = pl.pallas_call(
        functools.partial(inverse_kernel, cols, rows),
        out_shape=[shape((overall, overall)), shape((rows, 1, part))],
        in_specs=[SMEM] + [VMEM] * (cols + 3),
        out_specs=[VMEM] * 2,
        scratch_shapes=[pltpu.VMEM((overall, 1), F32)],
        compiler_params=params(16),
        name="inverse",
    )(place[:1], *inners, exact, noise_variance[None, :], innovation[None, :])
    weights_new = weights
    for k in range(rows):
        pairs = [
            (r * cols + c, c * rows + (r ^ k)) for r in range(rows) for c in range(cols)
        ]
        weights_new = weights_new + lax.ppermute(change, ("row", "col"), pairs)[k, 0]
    cov_new = pl.pallas_call(
        functools.partial(update_kernel, rows),
        out_shape=shape((height, width)),
        grid=(height // depth,),
        in_specs=[SMEM] + [VMEM] * (rows + 1) + [pl.BlockSpec((depth, width), lambda i: (i, 0))],
        out_specs=pl.BlockSpec((depth, width), lambda i: (i, 0)),
        scratch_shapes=[
            pltpu.VMEM((overall, height), BF16),
            pltpu.VMEM((overall, width), BF16),
            pltpu.VMEM((overall, height), F32),
        ],
        compiler_params=params(40),
        cost_estimate=estimate(2 * overall * height * width, 8 * height * width),
        name="update",
    )(place[:1], *routed, inverse, cov)
    return (weights_new, cov_new)


def solution(mesh):
    return jax.shard_map(
        on_device,
        mesh=mesh,
        in_specs=(
            P("row", "col"),
            P(("row", "col")),
            P("row", "col", None),
            P("row", "col", None),
            P("row", "col", None),
            P("row", "col"),
            P(),
            P("row", "col"),
            P("row"),
            P(),
            P(),
        ),
        out_specs=(P(("row", "col")), P("row", "col")),
        check_vma=False,
    )
```

```python
import functools
import math

import jax
import jax.numpy as jnp
from jax import lax
from jax.experimental import pallas as pl
from jax.experimental.pallas import tpu as pltpu
from jax.sharding import PartitionSpec as P

NS_ITERS = 5
FULL = lax.Precision.HIGHEST
F32 = jnp.float32
BF16 = jnp.bfloat16
EACH = (3, 2, 1)
EARLY, LATER = 2, 2

VMEM = pl.BlockSpec(memory_space=pltpu.VMEM)
SMEM = pl.BlockSpec(memory_space=pltpu.SMEM)


ANY = pl.BlockSpec(memory_space=pl.ANY)


def swap(block, axis, step):
    n = lax.axis_size(axis)
    return lax.ppermute(block, axis, [(i, i ^ step) for i in range(n)])


def gather_apart(block):
    return [block] + [swap(block, "col", k) for k in range(2, lax.axis_size("col"), 2)]


def gather(block):
    pieces = []
    for piece in gather_apart(block):
        pieces += [piece, swap(piece, "col", 1)]
    return pieces


def params(mib):
    return pltpu.CompilerParams(vmem_limit_bytes=mib * 2**20)


def shape(dims, kind=F32):
    return jax.ShapeDtypeStruct(dims, kind)


def resident(dims, kind=F32):
    return pltpu.VMEM(dims, kind)


def keep(block):
    return pltpu.with_memory_space_constraint(block, pltpu.VMEM)


def estimate(flops, moved):
    return pl.CostEstimate(flops=flops, bytes_accessed=moved, transcendentals=0)


def loads(source, first, targets, sems):
    copies = []
    for i, target in enumerate(targets):
        rows = target.shape[0]
        copies.append(
            pltpu.make_async_copy(source.at[pl.ds(first, rows), :], target, sems.at[i])
        )
        first += rows
    return copies


def pack_kernel(
    up_ref, act_ref, neighbors_ref, types_ref, gain_ref, sens_ref, frame_ref,
    packed_ref, near_ref, kinds_ref, scale_ref, masked_ref,
    up, act, sens, frame_of, sems,
):
    copies = [
        pltpu.make_async_copy(source, target, sems.at[i])
        for i, (source, target) in enumerate(
            (
                (up_ref, up),
                (act_ref, act),
                (neighbors_ref, near_ref),
                (types_ref, kinds_ref),
                (gain_ref, scale_ref),
                (sens_ref, sens),
                (frame_ref, frame_of),
            )
        )
    ]
    for copy in copies:
        copy.start()
    for copy in copies:
        copy.wait()
    width_out, width_in = up.shape[2], act.shape[2]
    packed_ref[:, :, pl.ds(0, width_out)] = up[...]
    packed_ref[:, :, pl.ds(width_out, width_in)] = act[...]
    measures, atoms = sens.shape
    frames = up.shape[0]
    index = lax.broadcasted_iota(jnp.int32, sens.shape, 0)
    frame = jnp.zeros(sens.shape, jnp.int32)
    for m in range(measures):
        frame = jnp.where(index == m, frame_of[m], frame)
    masked_ref[...] = jnp.concatenate(
        [jnp.where(frame == f, sens[...], 0.0) for f in range(frames)], axis=1
    )


def counts_kernel(first, near_ref, cov_ref, counts_ref, *refs):
    kept, (flipped, sems) = refs[:-2], refs[-2:]
    copies = loads(cov_ref, first, kept, sems)
    for copy in copies:
        copy.start()
    frames, atoms, slots = near_ref.shape
    lanes = frames * atoms
    whole, _ = counts_ref.shape
    flipped[...] = near_ref[...].reshape(lanes, slots).T
    chunk = min(256, whole)
    unroll = next(u for u in (6, 4, 3, 2, 1) if slots % u == 0)
    for base in range(0, whole, chunk):
        atom = lax.broadcasted_iota(jnp.int32, (chunk, lanes), 0) + base

        def step(s, total):
            for u in range(unroll):
                row = flipped[pl.ds(s * unroll + u, 1), :]
                total = jnp.where(atom == row, total + 1.0, total)
            return total

        total = lax.fori_loop(0, slots // unroll, step, jnp.zeros((chunk, lanes), F32))
        counts_ref[pl.ds(base, chunk), :] = total.astype(BF16)
    for copy in copies:
        copy.wait()


def adjoint_kernel(slots, width, *refs):
    counts_ref, kinds_ref, scale_ref, masked_ref = refs[:4]
    pieces, (out_ref, lookup) = refs[4:-2], refs[-2:]
    frames, atoms, _ = pieces[0].shape
    lanes = frames * atoms
    me = lax.axis_index("col")
    for k, piece in enumerate(pieces):
        start = pl.multiple_of((me ^ k) * atoms, atoms)
        for f in range(frames):
            lookup[f, pl.ds(start, atoms), :] = piece[f, :, pl.ds(0, width)]
    lane = lax.broadcasted_iota(jnp.int32, (1, lanes), 1)
    total = jnp.zeros((width, lanes), F32)
    for f in range(frames):
        part = lax.dot_general(
            lookup[f], counts_ref[...], (((0,), (0,)), ((), ())), preferred_element_type=F32
        )
        total = jnp.where((lane // atoms) == f, part, total)
    own = pieces[0][:, :, pl.ds(0, width)].reshape(lanes, width).astype(F32).T
    total = own + total * (1.0 / math.sqrt(slots))
    kinds = jnp.concatenate([kinds_ref[f : f + 1, :] for f in range(frames)], axis=1)
    gain = scale_ref[...].T
    scale = jnp.zeros((width, lanes), F32)
    for t in range(scale_ref.shape[0]):
        scale = jnp.where(kinds == t, gain[:, t : t + 1], scale)
    out_ref[pl.ds(0, width), :] = scale * total
    out_ref[pl.ds(width, masked_ref.shape[0]), :] = masked_ref[...]


def jacobian_kernel(count, row_peers, width_in, first_row, *refs):
    sides, packs, cov_ref = refs[:count], refs[count : 2 * count], refs[2 * count]
    outs = refs[2 * count + 1 : 2 * count + 2 + row_peers]
    kept = refs[2 * count + 2 + row_peers : -4]
    inputs, mixed, flat, sems = refs[-4:]
    copies = loads(cov_ref, first_row, kept, sems)
    for copy in copies:
        copy.start()
    row, col = lax.axis_index("row"), lax.axis_index("col")
    frames, atoms, _ = packs[0].shape
    lanes = frames * atoms
    measures = outs[0].shape[0]
    width_out = sides[0].shape[0] - measures
    for k, pack in enumerate(packs):
        inputs[pl.ds(k * lanes, lanes), :] = pack[:, :, pl.ds(width_out, width_in)].reshape(
            lanes, width_in
        )

    def block(out_ref, first):
        held = out_ref.shape[1] // width_in
        size = min(8, held)

        def group(g, carry):
            start = first + g * size
            for k, side in enumerate(sides):
                sens = side[pl.ds(width_out, measures), :]
                for b in range(size):
                    line = side[pl.ds(start + b, 1), :]
                    mixed[pl.ds(b * measures, measures), pl.ds(k * lanes, lanes)] = (
                        sens * line
                    ).astype(BF16)
            found = jnp.dot(
                mixed[pl.ds(0, size * measures), :], inputs[...], preferred_element_type=F32
            )
            for b in range(size):
                flat[:, pl.ds(b * width_in, width_in)] = found[
                    b * measures : (b + 1) * measures, :
                ]
            span = size * width_in
            at = g * span
            if span % 128 == 0:
                at = pl.multiple_of(at, 128)
            out_ref[:, pl.ds(at, span)] = flat[:, pl.ds(0, span)].astype(BF16)
            return carry

        if held == size:
            group(0, 0)
        else:
            lax.fori_loop(0, held // size, group, 0)

    for k in range(row_peers):
        block(outs[k], (row ^ k) * (outs[k].shape[1] // width_in))
    block(outs[row_peers], col * (outs[row_peers].shape[1] // width_in))
    for copy in copies:
        copy.wait()


def product_kernel(peers, depth, count, *refs):
    jac_refs, kept, cov_ref = refs[:peers], refs[peers : peers + count], refs[peers + count]
    refs = refs[peers + count + 1 :]
    whole_ref, sent, (jac, tiles, sems) = refs[0], refs[1:peers], refs[peers:]
    slots = tiles.shape[0]
    first = sum(part.shape[0] for part in kept)
    copies = [
        pltpu.make_async_copy(
            cov_ref.at[pl.ds(first + i * depth, depth), :], tiles.at[i % slots], sems.at[i % slots]
        )
        for i in range((cov_ref.shape[0] - first) // depth)
    ]
    for copy in copies[:slots]:
        copy.start()
    me = lax.axis_index("row")
    measures = jac_refs[0].shape[0]
    for k in range(peers):
        at = pl.multiple_of((me ^ k) * measures, measures)
        jac[pl.ds(at, measures), :] = jac_refs[k][...]
    whole_ref[...] = jnp.zeros_like(whole_ref)

    def add(left, block):
        high = block.astype(BF16)
        low = (block - high.astype(F32)).astype(BF16)
        whole_ref[...] += jnp.dot(left, high, preferred_element_type=F32) + jnp.dot(
            left, low, preferred_element_type=F32
        )

    base = 0
    for part in kept:

        def tile(i, carry, part=part, base=base):
            at = pl.multiple_of(i * depth, depth)
            left = jac[:, pl.ds(pl.multiple_of(base + at, depth), depth)]
            add(left, part[pl.ds(at, depth), :])
            return carry

        lax.fori_loop(0, part.shape[0] // depth, tile, 0)
        base += part.shape[0]
    for i, copy in enumerate(copies):
        copy.wait()
        add(jac[:, pl.ds(base + i * depth, depth)], tiles[i % slots])
        if i + slots < len(copies):
            copies[i + slots].start()
    for k in range(1, peers):
        at = pl.multiple_of((me ^ k) * measures, measures)
        sent[k - 1][...] = whole_ref[pl.ds(at, measures), :]


def inner_kernel(peers, *refs):
    jac_refs, whole_ref, inner_ref, jac = refs[:peers], refs[peers], refs[-2], refs[-1]
    me = lax.axis_index("row")
    measures = jac_refs[0].shape[0]
    for k in range(peers):
        at = pl.multiple_of((me ^ k) * measures, measures)
        jac[pl.ds(at, measures), :] = jac_refs[k][...].astype(F32)
    inner_ref[...] = lax.dot_general(
        whole_ref[...], jac[...], (((1,), (1,)), ((), ())), precision=FULL, preferred_element_type=F32
    )


def sum_kernel(peers, *refs):
    whole_ref, parts, inners = refs[0], refs[1:peers], refs[peers : 2 * peers]
    exact_ref, sent_ref = refs[2 * peers :]
    measures, width = exact_ref.shape
    me = lax.axis_index("row")
    total = whole_ref[pl.ds(pl.multiple_of(me * measures, measures), measures), :]
    for part in parts:
        total = total + part[...]
    exact_ref[...] = total
    sent_ref[:, pl.ds(0, width)] = total.astype(BF16)
    inner = inners[0][...]
    for k in range(1, peers):
        inner = inner + inners[k][...]
    high = inner.astype(BF16)
    low = (inner - high.astype(F32)).astype(BF16)
    overall = inner.shape[0]
    sent_ref[:, pl.ds(width, 2 * overall * peers)] = jnp.concatenate(
        [
            half[q * measures : (q + 1) * measures, :]
            for half in (high, low)
            for q in range(peers)
        ],
        axis=1,
    )


def route_kernel(peers, width, *refs):
    pieces, outs, inner_ref, held = refs[: -peers - 2], refs[-peers - 2 : -2], refs[-2], refs[-1]
    row, col = lax.axis_index("row"), lax.axis_index("col")
    count = len(pieces)
    per_block = count // peers
    measures = pieces[0].shape[0]
    overall = inner_ref.shape[0]
    total = jnp.zeros((measures, overall * peers), F32)
    for k, piece in enumerate(pieces):
        held[(col // 2) ^ k] = piece[:, pl.ds(0, width)]
        total = total + piece[:, pl.ds(width, overall * peers)].astype(F32)
        total = total + piece[:, pl.ds(width + overall * peers, overall * peers)].astype(F32)
    for q in range(peers):
        inner_ref[pl.ds(q * measures, measures), :] = total[:, q * overall : (q + 1) * overall]
    for k in range(peers):
        for p in range(per_block):
            outs[k][:, pl.ds(p * width, width)] = held[(row ^ k) * per_block + p]
        outs[k][:, pl.ds(per_block * width, width)] = pieces[0][:, pl.ds(0, width)]


def inverse_kernel(peers, *refs):
    inner_refs = refs[:2]
    exact_ref, noise_ref, innovation_ref, inverse_ref, change_ref, weight = refs[2:]
    row = lax.axis_index("row")
    overall = inverse_ref.shape[0]
    measures, width = exact_ref.shape
    inner = inner_refs[0][...] + inner_refs[1][...]
    down = lax.broadcasted_iota(jnp.int32, (overall, overall), 0)
    across = lax.broadcasted_iota(jnp.int32, (overall, overall), 1)
    diagonal = down == across
    inner = inner + jnp.where(diagonal, noise_ref[...], 0.0)
    scale = 1.0 / jnp.max(jnp.sum(jnp.abs(inner), axis=1, keepdims=True), axis=0, keepdims=True)
    inverse = jnp.where(diagonal, scale, 0.0)
    for _ in range(NS_ITERS):
        left = jnp.dot(inverse, inner, precision=FULL, preferred_element_type=F32)
        inverse = 2.0 * inverse - jnp.dot(left, inverse, precision=FULL, preferred_element_type=F32)
    inverse_ref[...] = inverse
    weight[...] = jnp.sum(inverse * innovation_ref[...], axis=1, keepdims=True)
    mine = weight[pl.ds(pl.multiple_of(row * measures, measures), measures), :]
    change = jnp.sum(exact_ref[...] * mine, axis=0, keepdims=True)
    part = width // peers
    for q in range(peers):
        change_ref[row ^ q] = change[:, q * part : (q + 1) * part]


def merge_kernel(*refs):
    pieces, half_ref, right_ref = refs[:-2], refs[-2], refs[-1]
    me = lax.axis_index("row")
    measures = pieces[0].shape[0]
    span, width = half_ref.shape[1], right_ref.shape[1]
    for k, piece in enumerate(pieces):
        at = pl.multiple_of((me ^ k) * measures, measures)
        half_ref[pl.ds(at, measures), :] = piece[:, pl.ds(0, span)]
        right_ref[pl.ds(at, measures), :] = piece[:, pl.ds(span, width)]


def update_kernel(mine_ref, other_ref, right_ref, inverse_ref, *refs):
    kept, (cov_ref, out_ref, left, staged) = refs[:-4], refs[-4:]
    step = pl.program_id(0)
    depth, width = out_ref.shape
    height = left.shape[1]

    @pl.when(step == 0)
    def _():
        core = lax.axis_index("col") % 2
        for p in range(height // (2 * width)):
            part = pl.ds(p * width, width)
            here = mine_ref[:, part].astype(F32)
            there = other_ref[:, part].astype(F32)
            staged[:, pl.ds(2 * p * width, width)] = jnp.where(core == 0, here, there)
            staged[:, pl.ds((2 * p + 1) * width, width)] = jnp.where(core == 0, there, here)
        left[...] = lax.dot_general(
            inverse_ref[...],
            staged[...],
            (((0,), (0,)), ((), ())),
            precision=FULL,
            preferred_element_type=F32,
        ).astype(BF16)

    gain = left[:, pl.ds(pl.multiple_of(step * depth, depth), depth)]
    change = lax.dot_general(
        gain, right_ref[...], (((0,), (0,)), ((), ())), preferred_element_type=F32
    )
    first = 0
    for part in kept:
        held = part.shape[0] // depth

        @pl.when((step >= first) & (step < first + held))
        def _(part=part, first=first):
            at = pl.multiple_of((step - first) * depth, depth)
            out_ref[...] = part[pl.ds(at, depth), :] - change

        first += held

    @pl.when(step >= first)
    def _():
        out_ref[...] = cov_ref[...] - change


def on_device(
    cov,
    weights,
    act,
    upstream,
    neighbors,
    types,
    type_gain,
    sens,
    frame_for_measure,
    noise_variance,
    innovation,
):
    rows, cols = lax.axis_size("row"), lax.axis_size("col")
    frames, atoms, width_in = act.shape
    width_out = upstream.shape[2]
    slots = neighbors.shape[2]
    lanes = frames * atoms
    measures = sens.shape[0]
    overall = measures * rows
    height, width = cov.shape
    part = weights.shape[0]
    dma = pltpu.SemaphoreType.DMA
    depth = next(d for d in (256, 128) if height % d == 0)
    tiles = height // depth
    each = next(n for n in EACH if tiles % n == 0)
    segments = tiles // each
    held = resident((each * depth, width))
    early, later = segments * EARLY // 6, segments * LATER // 6
    last = tiles - (early + later) * each
    packed_width = width_out + -(-width_in // 128) * 128

    packed, near, kinds, scale, masked = pl.pallas_call(
        pack_kernel,
        out_shape=[
            shape((frames, atoms, packed_width), BF16),
            shape(neighbors.shape, jnp.int32),
            shape(types.shape, jnp.int32),
            shape(type_gain.shape),
            shape((measures, lanes)),
        ],
        in_specs=[ANY] * 7,
        out_specs=[VMEM] * 5,
        scratch_shapes=[
            pltpu.VMEM(upstream.shape, BF16),
            pltpu.VMEM(act.shape, BF16),
            pltpu.VMEM(sens.shape, F32),
            pltpu.SMEM(frame_for_measure.shape, jnp.int32),
            dma((7,)),
        ],
        compiler_params=params(3),
        name="pack",
    )(upstream, act, neighbors, types, type_gain, sens, frame_for_measure)
    packs = gather(packed)
    counts, *kept = pl.pallas_call(
        functools.partial(counts_kernel, 0),
        out_shape=[shape((atoms * cols, lanes), BF16)] + [held] * early,
        in_specs=[VMEM, ANY],
        out_specs=[VMEM] * (1 + early),
        scratch_shapes=[pltpu.VMEM((slots, lanes), jnp.int32), dma((early,))],
        compiler_params=params(3),
        cost_estimate=estimate(10**9, 4 * early * each * depth * width),
        name="counts",
    )(near, cov)
    side = pl.pallas_call(
        functools.partial(adjoint_kernel, slots, width_out),
        out_shape=shape((width_out + measures, lanes)),
        in_specs=[VMEM] * (4 + cols),
        out_specs=VMEM,
        scratch_shapes=[pltpu.VMEM((frames, atoms * cols, width_out), BF16)],
        compiler_params=params(3),
        name="adjoint",
    )(counts, kinds, scale, masked, *packs)
    sides = gather(side)
    jacs = pl.pallas_call(
        functools.partial(jacobian_kernel, cols, rows, width_in, early * each * depth),
        out_shape=[shape((measures, height), BF16)] * rows
        + [shape((measures, width), BF16)]
        + [held] * later,
        in_specs=[VMEM] * (2 * cols) + [ANY],
        out_specs=[VMEM] * (rows + 1 + later),
        scratch_shapes=[
            pltpu.VMEM((cols * lanes, width_in), BF16),
            pltpu.VMEM((8 * measures, cols * lanes), BF16),
            pltpu.VMEM((measures, 8 * width_in), F32),
            dma((later,)),
        ],
        compiler_params=params(5),
        name="jacobian",
    )(*sides, *packs, cov)
    kept += jacs[rows + 1 :]
    jac_rows = [jacs[0]] + [swap(jacs[k], "row", k) for k in range(1, rows)]
    jac_cols = [jacs[rows]] + [swap(jacs[rows], "row", k) for k in range(1, rows)]

    whole, *parts = pl.pallas_call(
        functools.partial(product_kernel, rows, depth, early + later),
        out_shape=[shape((overall, width))]
        + [shape((measures, width))] * (rows - 1),
        in_specs=[VMEM] * (rows + early + later) + [ANY],
        out_specs=[VMEM] * rows,
        scratch_shapes=[pltpu.VMEM((overall, height), BF16),
            pltpu.VMEM((2, depth, width), F32),
            dma((2,)),
        ],
        compiler_params=params(14),
        cost_estimate=estimate(4 * overall * height * width, 4 * last * depth * width),
        name="product",
    )(*jac_rows, *map(keep, kept), cov)
    parts = [swap(block, "row", k + 1) for k, block in enumerate(parts)]
    inner = pl.pallas_call(
        functools.partial(inner_kernel, rows),
        out_shape=shape((overall, overall)),
        in_specs=[VMEM] * (rows + 1),
        out_specs=VMEM,
        scratch_shapes=[pltpu.VMEM((overall, width), F32)],
        compiler_params=params(5),
        name="inner",
    )(*jac_cols, whole)
    inners = [inner] + [swap(inner, "row", k) for k in range(1, rows)]
    exact, sent = pl.pallas_call(
        functools.partial(sum_kernel, rows),
        out_shape=[
            shape((measures, width)),
            shape((measures, width + 2 * overall * rows), BF16),
        ],
        in_specs=[VMEM] * (2 * rows),
        out_specs=[VMEM] * 2,
        compiler_params=params(3),
        name="sum",
    )(whole, *parts, *inners)
    sents = gather_apart(sent)
    span = height // 2
    *routed, inner = pl.pallas_call(
        functools.partial(route_kernel, rows, width),
        out_shape=[shape((measures, span + width), BF16)] * rows + [shape((overall, overall))],
        in_specs=[VMEM] * (cols // 2),
        out_specs=[VMEM] * (rows + 1),
        scratch_shapes=[pltpu.VMEM((cols // 2, measures, width), BF16)],
        compiler_params=params(3),
        name="route",
    )(*sents)
    routed = [routed[0]] + [swap(routed[k], "row", k) for k in range(1, rows)]
    inverse, change = pl.pallas_call(
        functools.partial(inverse_kernel, rows),
        out_shape=[shape((overall, overall)), shape((rows, 1, part))],
        in_specs=[VMEM] * 5,
        out_specs=[VMEM] * 2,
        scratch_shapes=[pltpu.VMEM((overall, 1), F32)],
        compiler_params=params(3),
        name="inverse",
    )(inner, swap(inner, "col", 1), exact, noise_variance[None, :], innovation[None, :])
    half, right = pl.pallas_call(
        merge_kernel,
        out_shape=[shape((overall, span), BF16), shape((overall, width), BF16)],
        in_specs=[VMEM] * rows,
        out_specs=[VMEM] * 2,
        compiler_params=params(3),
        name="merge",
    )(*routed)
    other = swap(half, "col", 1)
    weights_new = weights
    for k in range(rows):
        pairs = [
            (r * cols + c, c * rows + (r ^ k)) for r in range(rows) for c in range(cols)
        ]
        weights_new = weights_new + lax.ppermute(change, ("row", "col"), pairs)[k, 0]
    skipped = (early + later) * each
    cov_new = pl.pallas_call(
        update_kernel,
        out_shape=shape((height, width)),
        grid=(tiles,),
        in_specs=[VMEM] * (4 + early + later)
        + [pl.BlockSpec((depth, width), lambda i: (jnp.maximum(i, skipped), 0))],
        out_specs=pl.BlockSpec((depth, width), lambda i: (i, 0)),
        scratch_shapes=[
            pltpu.VMEM((overall, height), BF16),
            pltpu.VMEM((overall, height), F32),
        ],
        compiler_params=params(14),
        cost_estimate=estimate(2 * overall * height * width, 4 * height * width),
        name="update",
    )(half, other, right, inverse, *map(keep, kept), cov)
    return (weights_new, cov_new)


def solution(mesh):
    return jax.shard_map(
        on_device,
        mesh=mesh,
        in_specs=(
            P("row", "col"),
            P(("row", "col")),
            P("row", "col", None),
            P("row", "col", None),
            P("row", "col", None),
            P("row", "col"),
            P(),
            P("row", "col"),
            P("row"),
            P(),
            P(),
        ),
        out_specs=(P(("row", "col")), P("row", "col")),
        check_vma=False,
    )
```

```python
import functools
import math

import jax
import jax.numpy as jnp
from jax import lax
from jax.experimental import pallas as pl
from jax.experimental.pallas import tpu as pltpu
from jax.sharding import PartitionSpec as P


NS_ITERS = 5
FULL = lax.Precision.HIGHEST
F32 = jnp.float32
BF16 = jnp.bfloat16
EACH = (3, 2, 1)
EARLY, LATER = 2, 2

VMEM = pl.BlockSpec(memory_space=pltpu.VMEM)
SMEM = pl.BlockSpec(memory_space=pltpu.SMEM)


ANY = pl.BlockSpec(memory_space=pl.ANY)


def swap(block, axis, step):
    n = lax.axis_size(axis)
    return lax.ppermute(block, axis, [(i, i ^ step) for i in range(n)])


def gather_apart(block):
    return [block] + [swap(block, "col", k) for k in range(2, lax.axis_size("col"), 2)]


def exchange(blocks):
    return [blocks[0]] + [swap(block, "row", k) for k, block in enumerate(blocks) if k]


def gather(block):
    pieces = []
    for piece in gather_apart(block):
        pieces += [piece, swap(piece, "col", 1)]
    return pieces


def params(mib):
    return pltpu.CompilerParams(vmem_limit_bytes=mib * 2**20)


def shape(dims, kind=F32):
    return jax.ShapeDtypeStruct(dims, kind)


def resident(dims, kind=F32):
    return pltpu.VMEM(dims, kind)


def outside(block):
    return pltpu.with_memory_space_constraint(block, pltpu.HBM)


def keep(block):
    return pltpu.with_memory_space_constraint(block, pltpu.VMEM)


def estimate(flops, moved):
    return pl.CostEstimate(flops=flops, bytes_accessed=moved, transcendentals=0)


def loads(source, first, targets, sems):
    copies = []
    for i, target in enumerate(targets):
        rows = target.shape[0]
        copies.append(
            pltpu.make_async_copy(source.at[pl.ds(first, rows), :], target, sems.at[i])
        )
        first += rows
    return copies


def pack_kernel(
    up_ref, act_ref, neighbors_ref, types_ref, gain_ref, sens_ref, frame_ref,
    packed_ref, near_ref, kinds_ref, scale_ref, masked_ref,
    up, act, sens, frame_of, sems,
):
    copies = [
        pltpu.make_async_copy(source, target, sems.at[i])
        for i, (source, target) in enumerate(
            (
                (up_ref, up),
                (act_ref, act),
                (neighbors_ref, near_ref),
                (types_ref, kinds_ref),
                (gain_ref, scale_ref),
                (sens_ref, sens),
                (frame_ref, frame_of),
            )
        )
    ]
    for copy in copies:
        copy.start()
    for copy in copies:
        copy.wait()
    width_out, width_in = up.shape[2], act.shape[2]
    packed_ref[:, :, pl.ds(0, width_out)] = up[...]
    packed_ref[:, :, pl.ds(width_out, width_in)] = act[...]
    measures, _ = sens.shape
    frames = up.shape[0]
    index = lax.broadcasted_iota(jnp.int32, sens.shape, 0)
    frame = jnp.zeros(sens.shape, jnp.int32)
    for m in range(measures):
        frame = jnp.where(index == m, frame_of[m], frame)
    masked_ref[...] = jnp.concatenate(
        [jnp.where(frame == f, sens[...], 0.0) for f in range(frames)], axis=1
    )


def counts_kernel(first, near_ref, cov_ref, counts_ref, *refs):
    kept, (flipped, sems) = refs[:-2], refs[-2:]
    copies = loads(cov_ref, first, kept, sems)
    for copy in copies:
        copy.start()
    frames, atoms, slots = near_ref.shape
    lanes = frames * atoms
    whole, _ = counts_ref.shape
    flipped[...] = near_ref[...].reshape(lanes, slots).T
    chunk = min(256, whole)
    unroll = next(u for u in (6, 4, 3, 2, 1) if slots % u == 0)
    for base in range(0, whole, chunk):
        atom = lax.broadcasted_iota(jnp.int32, (chunk, lanes), 0) + base

        def step(s, total):
            for u in range(unroll):
                row = flipped[pl.ds(s * unroll + u, 1), :]
                total = jnp.where(atom == row, total + 1.0, total)
            return total

        total = lax.fori_loop(0, slots // unroll, step, jnp.zeros((chunk, lanes), F32))
        counts_ref[pl.ds(base, chunk), :] = total.astype(BF16)
    for copy in copies:
        copy.wait()


def adjoint_kernel(slots, width, *refs):
    counts_ref, kinds_ref, scale_ref, masked_ref = refs[:4]
    pieces, (out_ref, lookup) = refs[4:-2], refs[-2:]
    frames, atoms, _ = pieces[0].shape
    lanes = frames * atoms
    me = lax.axis_index("col")
    for k, piece in enumerate(pieces):
        start = pl.multiple_of((me ^ k) * atoms, atoms)
        for f in range(frames):
            lookup[f, pl.ds(start, atoms), :] = piece[f, :, pl.ds(0, width)]
    lane = lax.broadcasted_iota(jnp.int32, (1, lanes), 1)
    total = jnp.zeros((width, lanes), F32)
    for f in range(frames):
        part = lax.dot_general(
            lookup[f], counts_ref[...], (((0,), (0,)), ((), ())), preferred_element_type=F32
        )
        total = jnp.where((lane // atoms) == f, part, total)
    own = pieces[0][:, :, pl.ds(0, width)].reshape(lanes, width).astype(F32).T
    total = own + total * (1.0 / math.sqrt(slots))
    kinds = jnp.concatenate([kinds_ref[f : f + 1, :] for f in range(frames)], axis=1)
    gain = scale_ref[...].T
    scale = jnp.zeros((width, lanes), F32)
    for t in range(scale_ref.shape[0]):
        scale = jnp.where(kinds == t, gain[:, t : t + 1], scale)
    out_ref[pl.ds(0, width), :] = scale * total
    out_ref[pl.ds(width, masked_ref.shape[0]), :] = masked_ref[...]


def jacobian_kernel(count, peers, width_in, skip, span, first_row, *refs):
    sides, packs, cov_ref = refs[:count], refs[count : 2 * count], refs[2 * count]
    outs, kept = refs[2 * count + 1 : 2 * count + 1 + peers], refs[2 * count + 1 + peers : -4]
    inputs, mixed, flat, sems = refs[-4:]
    copies = loads(cov_ref, first_row, kept, sems)
    for copy in copies:
        copy.start()
    row, col = lax.axis_index("row"), lax.axis_index("col")
    frames, atoms, _ = packs[0].shape
    lanes = frames * atoms
    measures = outs[0].shape[0]
    width_out = sides[0].shape[0] - measures
    for k, pack in enumerate(packs):
        inputs[pl.ds(k * lanes, lanes), :] = pack[:, :, pl.ds(width_out, width_in)].reshape(
            lanes, width_in
        )

    def block(targets, base, held, first):
        size = min(8, held)

        def group(g, carry):
            start = first + g * size
            for k, side in enumerate(sides):
                sens = side[pl.ds(width_out, measures), :]
                for b in range(size):
                    line = side[pl.ds(start + b, 1), :]
                    mixed[pl.ds(b * measures, measures), pl.ds(k * lanes, lanes)] = (
                        sens * line
                    ).astype(BF16)
            found = jnp.dot(
                mixed[pl.ds(0, size * measures), :], inputs[...], preferred_element_type=F32
            )
            for b in range(size):
                flat[:, pl.ds(b * width_in, width_in)] = found[
                    b * measures : (b + 1) * measures, :
                ]
            reach = size * width_in
            at = base + g * reach
            if reach % 128 == 0:
                at = pl.multiple_of(at, 128)
            for target in targets:
                target[:, pl.ds(at, reach)] = flat[:, pl.ds(0, reach)].astype(BF16)
            return carry

        if held == size:
            group(0, 0)
        else:
            lax.fori_loop(0, held // size, group, 0)

    per_row = width_out // peers
    for k in range(peers):
        block([outs[k]], 0, span // width_in, (row ^ k) * per_row + skip // width_in)
    side_span = (outs[0].shape[1] - span) // width_in
    if side_span:
        block(outs, span, side_span, col * side_span)
    for copy in copies:
        copy.wait()


def multiply(whole_ref, jac, base, depth, part, tiles):
    def tile(i, carry):
        at = i * depth
        if not isinstance(i, int):
            at = pl.multiple_of(at, depth)
        left = jac[:, pl.ds(base + at, depth)]
        block = part[pl.ds(at, depth), :]
        high = block.astype(BF16)
        low = (block - high.astype(F32)).astype(BF16)
        whole_ref[...] += jnp.dot(left, high, preferred_element_type=F32) + jnp.dot(
            left, low, preferred_element_type=F32
        )
        return carry

    if tiles == 1:
        tile(0, 0)
    else:
        lax.fori_loop(0, tiles, tile, 0)


def arrange(target, sources, start, span):
    me = lax.axis_index("row")
    for k, source in enumerate(sources):
        measures = source.shape[0]
        at = pl.multiple_of((me ^ k) * measures, measures)
        target[pl.ds(at, measures), :] = source[:, pl.ds(start, span)].astype(target.dtype)


def product_first_kernel(peers, depth, *refs):
    jac_refs, kept, (whole_ref, jac) = refs[:peers], refs[peers:-2], refs[-2:]
    arrange(jac, jac_refs, 0, jac.shape[1])
    whole_ref[...] = jnp.zeros_like(whole_ref)
    base = 0
    for part in kept:
        multiply(whole_ref, jac, base, depth, part, part.shape[0] // depth)
        base += part.shape[0]


def product_last_kernel(peers, depth, count, *refs):
    jac_refs, begun_ref, kept = refs[:peers], refs[peers], refs[peers + 1 : peers + 1 + count]
    cov_ref = refs[peers + 1 + count]
    outs, (jac, side, whole, tiles, sems) = refs[peers + 2 + count : -5], refs[-5:]
    slots = tiles.shape[0]
    span = jac.shape[1]
    held = sum(part.shape[0] for part in kept)
    start = cov_ref.shape[0] - span + held
    copies = [
        pltpu.make_async_copy(
            cov_ref.at[pl.ds(start + i * depth, depth), :], tiles.at[i % slots], sems.at[i % slots]
        )
        for i in range((span - held) // depth)
    ]
    for copy in copies[:slots]:
        copy.start()
    arrange(jac, jac_refs, 0, span)
    arrange(side, jac_refs, span, side.shape[1])
    whole[...] = begun_ref[...]
    base = 0
    for part in kept:
        multiply(whole, jac, base, depth, part, part.shape[0] // depth)
        base += part.shape[0]
    for i, copy in enumerate(copies):
        copy.wait()
        multiply(whole, jac, base + i * depth, depth, tiles.at[i % slots], 1)
        if i + slots < len(copies):
            copies[i + slots].start()
    inner = lax.dot_general(
        whole[...], side[...], (((1,), (1,)), ((), ())), precision=FULL, preferred_element_type=F32
    )
    me = lax.axis_index("row")
    overall, width = whole.shape
    measures = overall // peers
    for k in range(peers):
        at = pl.multiple_of((me ^ k) * measures, measures)
        outs[k][:, pl.ds(0, width)] = whole[pl.ds(at, measures), :]
        outs[k][:, pl.ds(width, overall * peers)] = jnp.concatenate(
            [inner[q * measures : (q + 1) * measures, :] for q in range(peers)], axis=1
        )


def sum_kernel(*refs):
    parts, (exact_ref, sent_ref) = refs[:-2], refs[-2:]
    width = exact_ref.shape[1]
    total = parts[0][...]
    for part in parts[1:]:
        total = total + part[...]
    exact_ref[...] = total[:, :width]
    sent_ref[:, pl.ds(0, width)] = total[:, :width].astype(BF16)
    inner = total[:, width:]
    high = inner.astype(BF16)
    sent_ref[:, pl.ds(width, inner.shape[1])] = high
    sent_ref[:, pl.ds(width + inner.shape[1], inner.shape[1])] = (
        inner - high.astype(F32)
    ).astype(BF16)


def route_kernel(peers, width, *refs):
    pieces, outs, inner_ref, held = refs[: -peers - 2], refs[-peers - 2 : -2], refs[-2], refs[-1]
    row, col = lax.axis_index("row"), lax.axis_index("col")
    count = len(pieces)
    per_block = count // peers
    measures = pieces[0].shape[0]
    overall = inner_ref.shape[0]
    total = jnp.zeros((measures, overall * peers), F32)
    for k, piece in enumerate(pieces):
        held[(col // 2) ^ k] = piece[:, pl.ds(0, width)]
        total = total + piece[:, pl.ds(width, overall * peers)].astype(F32)
        total = total + piece[:, pl.ds(width + overall * peers, overall * peers)].astype(F32)
    for q in range(peers):
        inner_ref[pl.ds(q * measures, measures), :] = total[:, q * overall : (q + 1) * overall]
    for k in range(peers):
        for p in range(per_block):
            outs[k][:, pl.ds(p * width, width)] = held[(row ^ k) * per_block + p]
        outs[k][:, pl.ds(per_block * width, width)] = pieces[0][:, pl.ds(0, width)]


def inverse_kernel(peers, *refs):
    inner_refs = refs[:2]
    exact_ref, noise_ref, innovation_ref, inverse_ref, change_ref, weight = refs[2:]
    row = lax.axis_index("row")
    overall = inverse_ref.shape[0]
    measures, width = exact_ref.shape
    inner = inner_refs[0][...] + inner_refs[1][...]
    down = lax.broadcasted_iota(jnp.int32, (overall, overall), 0)
    across = lax.broadcasted_iota(jnp.int32, (overall, overall), 1)
    diagonal = down == across
    inner = inner + jnp.where(diagonal, noise_ref[...], 0.0)
    scale = 1.0 / jnp.max(jnp.sum(jnp.abs(inner), axis=1, keepdims=True), axis=0, keepdims=True)
    inverse = jnp.where(diagonal, scale, 0.0)
    for _ in range(NS_ITERS):
        left = jnp.dot(inverse, inner, precision=FULL, preferred_element_type=F32)
        inverse = 2.0 * inverse - jnp.dot(left, inverse, precision=FULL, preferred_element_type=F32)
    inverse_ref[...] = inverse
    weight[...] = jnp.sum(inverse * innovation_ref[...], axis=1, keepdims=True)
    mine = weight[pl.ds(pl.multiple_of(row * measures, measures), measures), :]
    change = jnp.sum(exact_ref[...] * mine, axis=0, keepdims=True)
    part = width // peers
    for q in range(peers):
        change_ref[row ^ q] = change[:, q * part : (q + 1) * part]


def merge_kernel(*refs):
    pieces, half_ref, right_ref = refs[:-2], refs[-2], refs[-1]
    me = lax.axis_index("row")
    measures = pieces[0].shape[0]
    span, width = half_ref.shape[1], right_ref.shape[1]
    for k, piece in enumerate(pieces):
        at = pl.multiple_of((me ^ k) * measures, measures)
        half_ref[pl.ds(at, measures), :] = piece[:, pl.ds(0, span)]
        right_ref[pl.ds(at, measures), :] = piece[:, pl.ds(span, width)]


def update_kernel(mine_ref, other_ref, right_ref, inverse_ref, *refs):
    kept, (cov_ref, out_ref, left, staged) = refs[:-4], refs[-4:]
    step = pl.program_id(0)
    depth, width = out_ref.shape
    height = left.shape[1]

    @pl.when(step == 0)
    def _():
        core = lax.axis_index("col") % 2
        for p in range(height // (2 * width)):
            part = pl.ds(p * width, width)
            here = mine_ref[:, part].astype(F32)
            there = other_ref[:, part].astype(F32)
            staged[:, pl.ds(2 * p * width, width)] = jnp.where(core == 0, here, there)
            staged[:, pl.ds((2 * p + 1) * width, width)] = jnp.where(core == 0, there, here)
        left[...] = lax.dot_general(
            inverse_ref[...],
            staged[...],
            (((0,), (0,)), ((), ())),
            precision=FULL,
            preferred_element_type=F32,
        ).astype(BF16)

    gain = left[:, pl.ds(pl.multiple_of(step * depth, depth), depth)]
    change = lax.dot_general(
        gain, right_ref[...], (((0,), (0,)), ((), ())), preferred_element_type=F32
    )
    first = 0
    for part in kept:
        held = part.shape[0] // depth

        @pl.when((step >= first) & (step < first + held))
        def _(part=part, first=first):
            at = pl.multiple_of((step - first) * depth, depth)
            out_ref[...] = part[pl.ds(at, depth), :] - change

        first += held

    @pl.when(step >= first)
    def _():
        out_ref[...] = cov_ref[...] - change


def on_device(
    cov,
    weights,
    act,
    upstream,
    neighbors,
    types,
    type_gain,
    sens,
    frame_for_measure,
    noise_variance,
    innovation,
):
    rows, cols = lax.axis_size("row"), lax.axis_size("col")
    frames, atoms, width_in = act.shape
    width_out = upstream.shape[2]
    slots = neighbors.shape[2]
    lanes = frames * atoms
    measures = sens.shape[0]
    overall = measures * rows
    height, width = cov.shape
    part = weights.shape[0]
    dma = pltpu.SemaphoreType.DMA
    depth = next(d for d in (256, 128) if height % d == 0)
    tiles = height // depth
    each = next(n for n in EACH if tiles % n == 0)
    segments = tiles // each
    held = resident((each * depth, width))
    early, later = segments * EARLY // 6, segments * LATER // 6
    packed_width = width_out + -(-width_in // 128) * 128

    packed, near, kinds, scale, masked = pl.pallas_call(
        pack_kernel,
        out_shape=[
            shape((frames, atoms, packed_width), BF16),
            shape(neighbors.shape, jnp.int32),
            shape(types.shape, jnp.int32),
            shape(type_gain.shape),
            shape((measures, lanes)),
        ],
        in_specs=[ANY] * 7,
        out_specs=[VMEM] * 5,
        scratch_shapes=[
            pltpu.VMEM(upstream.shape, BF16),
            pltpu.VMEM(act.shape, BF16),
            pltpu.VMEM(sens.shape, F32),
            pltpu.SMEM(frame_for_measure.shape, jnp.int32),
            dma((7,)),
        ],
        compiler_params=params(3),
        name="pack",
    )(*map(outside, (upstream, act, neighbors, types, type_gain, sens, frame_for_measure)))
    packs = gather(packed)
    counts, *kept = pl.pallas_call(
        functools.partial(counts_kernel, 0),
        out_shape=[shape((atoms * cols, lanes), BF16)] + [held] * early,
        in_specs=[VMEM, ANY],
        out_specs=[VMEM] * (1 + early),
        scratch_shapes=[pltpu.VMEM((slots, lanes), jnp.int32), dma((early,))],
        compiler_params=params(3),
        cost_estimate=estimate(3 * 10**9, 4 * early * each * depth * width),
        name="counts",
    )(near, outside(cov))
    side = pl.pallas_call(
        functools.partial(adjoint_kernel, slots, width_out),
        out_shape=shape((width_out + measures, lanes)),
        in_specs=[VMEM] * (4 + cols),
        out_specs=VMEM,
        scratch_shapes=[pltpu.VMEM((frames, atoms * cols, width_out), BF16)],
        compiler_params=params(3),
        name="adjoint",
    )(counts, kinds, scale, masked, *packs)
    sides = gather(side)
    part_a = tiles // 2 // each * each * depth
    part_b = height - part_a
    kept = list(kept)
    jacs = []
    for skip, size, extra, loaded in (
        (0, part_a, 0, later // 2),
        (part_a, part_b, width, later - later // 2),
    ):
        found = pl.pallas_call(
            functools.partial(
                jacobian_kernel, cols, rows, width_in, skip, size, len(kept) * each * depth
            ),
            out_shape=[shape((measures, size + extra), BF16)] * rows + [held] * loaded,
            in_specs=[VMEM] * (2 * cols) + [ANY],
            out_specs=[VMEM] * (rows + loaded),
            scratch_shapes=[
                pltpu.VMEM((cols * lanes, width_in), BF16),
                pltpu.VMEM((8 * measures, cols * lanes), BF16),
                pltpu.VMEM((measures, 8 * width_in), F32),
                dma((max(1, loaded),)),
            ],
            compiler_params=params(5),
            cost_estimate=estimate(3 * 10**9, 4 * loaded * each * depth * width),
            name="jacobian_last" if skip else "jacobian_first",
        )(*sides, *packs, outside(cov))
        kept += found[rows:]
        jacs.append(exchange(found[:rows]))
    first = part_a // (each * depth)
    begun = pl.pallas_call(
        functools.partial(product_first_kernel, rows, depth),
        out_shape=shape((overall, width)),
        in_specs=[VMEM] * (rows + first),
        out_specs=VMEM,
        scratch_shapes=[pltpu.VMEM((overall, part_a), BF16)],
        compiler_params=params(9),
        cost_estimate=estimate(8 * overall * part_a * width, 4 * part_a * width),
        name="product_first",
    )(*jacs[0], *map(keep, kept[:first]))
    rest = len(kept) - first
    parts = pl.pallas_call(
        functools.partial(product_last_kernel, rows, depth, rest),
        out_shape=[shape((measures, width + overall * rows))] * rows,
        in_specs=[VMEM] * (rows + 1 + rest) + [ANY],
        out_specs=[VMEM] * rows,
        scratch_shapes=[
            pltpu.VMEM((overall, part_b), BF16),
            pltpu.VMEM((overall, width), F32),
            pltpu.VMEM((overall, width), F32),
            pltpu.VMEM((2, depth, width), F32),
            dma((2,)),
        ],
        compiler_params=params(14),
        cost_estimate=estimate(8 * overall * part_b * width, 4 * part_b * width),
        name="product_last",
    )(*jacs[1], begun, *map(keep, kept[first:]), outside(cov))
    parts = exchange(parts)
    exact, sent = pl.pallas_call(
        sum_kernel,
        out_shape=[
            shape((measures, width)),
            shape((measures, width + 2 * overall * rows), BF16),
        ],
        in_specs=[VMEM] * rows,
        out_specs=[VMEM] * 2,
        compiler_params=params(3),
        name="sum",
    )(*parts)
    sents = gather_apart(sent)
    span = height // 2
    *routed, inner = pl.pallas_call(
        functools.partial(route_kernel, rows, width),
        out_shape=[shape((measures, span + width), BF16)] * rows + [shape((overall, overall))],
        in_specs=[VMEM] * (cols // 2),
        out_specs=[VMEM] * (rows + 1),
        scratch_shapes=[pltpu.VMEM((cols // 2, measures, width), BF16)],
        compiler_params=params(3),
        name="route",
    )(*sents)
    routed = exchange(routed)
    shared = swap(inner, "col", 1)
    inverse, change = pl.pallas_call(
        functools.partial(inverse_kernel, rows),
        out_shape=[shape((overall, overall)), shape((rows, 1, part))],
        in_specs=[VMEM] * 5,
        out_specs=[VMEM] * 2,
        scratch_shapes=[pltpu.VMEM((overall, 1), F32)],
        compiler_params=params(3),
        name="inverse",
    )(inner, shared, exact, noise_variance[None, :], innovation[None, :])
    half, right = pl.pallas_call(
        merge_kernel,
        out_shape=[shape((overall, span), BF16), shape((overall, width), BF16)],
        in_specs=[VMEM] * rows,
        out_specs=[VMEM] * 2,
        compiler_params=params(3),
        name="merge",
    )(*routed)
    other = swap(half, "col", 1)
    weights_new = weights
    for k in range(rows):
        pairs = [
            (r * cols + c, c * rows + (r ^ k)) for r in range(rows) for c in range(cols)
        ]
        moved = lax.ppermute(change, ("row", "col"), pairs)
        weights_new = weights_new + moved[k, 0]
    skipped = (early + later) * each
    cov_new = pl.pallas_call(
        update_kernel,
        out_shape=shape((height, width)),
        grid=(tiles,),
        in_specs=[VMEM] * (4 + early + later)
        + [pl.BlockSpec((depth, width), lambda i: (jnp.maximum(i, skipped), 0))],
        out_specs=pl.BlockSpec((depth, width), lambda i: (i, 0)),
        scratch_shapes=[
            pltpu.VMEM((overall, height), BF16),
            pltpu.VMEM((overall, height), F32),
        ],
        compiler_params=params(14),
        cost_estimate=estimate(2 * overall * height * width, 4 * height * width),
        name="update",
    )(half, other, right, inverse, *map(keep, kept), outside(cov))
    return (weights_new, cov_new)


def solution(mesh):
    return jax.shard_map(
        on_device,
        mesh=mesh,
        in_specs=(
            P("row", "col"),
            P(("row", "col")),
            P("row", "col", None),
            P("row", "col", None),
            P("row", "col", None),
            P("row", "col"),
            P(),
            P("row", "col"),
            P("row"),
            P(),
            P(),
        ),
        out_specs=(P(("row", "col")), P("row", "col")),
        check_vma=False,
    )
```

```python
import functools
import math

import jax
import jax.numpy as jnp
from jax import lax
from jax.experimental import pallas as pl
from jax.experimental.pallas import tpu as pltpu
from jax.sharding import PartitionSpec as P


NS_ITERS = 5
FULL = lax.Precision.HIGHEST
F32 = jnp.float32
BF16 = jnp.bfloat16
EACH = (3, 2, 1)
EARLY, LATER = 3, 2
CUT = 768
THIN, SLOTS = 128, 4

VMEM = pl.BlockSpec(memory_space=pltpu.VMEM)
SMEM = pl.BlockSpec(memory_space=pltpu.SMEM)


ANY = pl.BlockSpec(memory_space=pl.ANY)


def swap(block, axis, step):
    n = lax.axis_size(axis)
    return lax.ppermute(block, axis, [(i, i ^ step) for i in range(n)])


def gather_apart(block):
    return [block] + [swap(block, "col", k) for k in range(2, lax.axis_size("col"), 2)]


def exchange(blocks):
    return [blocks[0]] + [swap(block, "row", k) for k, block in enumerate(blocks) if k]


def gather(block):
    pieces = []
    for piece in gather_apart(block):
        pieces += [piece, swap(piece, "col", 1)]
    return pieces


def params(mib):
    return pltpu.CompilerParams(vmem_limit_bytes=mib * 2**20)


def shape(dims, kind=F32):
    return jax.ShapeDtypeStruct(dims, kind)


def resident(dims, kind=F32):
    return pltpu.VMEM(dims, kind)


def outside(block):
    return pltpu.with_memory_space_constraint(block, pltpu.HBM)


def keep(block):
    return pltpu.with_memory_space_constraint(block, pltpu.VMEM)


def estimate(flops, moved):
    return pl.CostEstimate(flops=flops, bytes_accessed=moved, transcendentals=0)


def loads(source, first, targets, sems):
    copies = []
    for i, target in enumerate(targets):
        rows = target.shape[0]
        copies.append(
            pltpu.make_async_copy(source.at[pl.ds(first, rows), :], target, sems.at[i])
        )
        first += rows
    return copies


def pack_kernel(
    up_ref, act_ref, neighbors_ref, types_ref, gain_ref, sens_ref, frame_ref,
    packed_ref, near_ref, kinds_ref, scale_ref, masked_ref,
    up, act, sens, frame_of, sems,
):
    copies = [
        pltpu.make_async_copy(source, target, sems.at[i])
        for i, (source, target) in enumerate(
            (
                (up_ref, up),
                (act_ref, act),
                (neighbors_ref, near_ref),
                (types_ref, kinds_ref),
                (gain_ref, scale_ref),
                (sens_ref, sens),
                (frame_ref, frame_of),
            )
        )
    ]
    for copy in copies:
        copy.start()
    for copy in copies:
        copy.wait()
    width_out, width_in = up.shape[2], act.shape[2]
    packed_ref[:, :, pl.ds(0, width_out)] = up[...]
    packed_ref[:, :, pl.ds(width_out, width_in)] = act[...]
    measures, _ = sens.shape
    frames = up.shape[0]
    index = lax.broadcasted_iota(jnp.int32, sens.shape, 0)
    frame = jnp.zeros(sens.shape, jnp.int32)
    for m in range(measures):
        frame = jnp.where(index == m, frame_of[m], frame)
    masked_ref[...] = jnp.concatenate(
        [jnp.where(frame == f, sens[...], 0.0) for f in range(frames)], axis=1
    )


def counts_kernel(first, near_ref, cov_ref, counts_ref, *refs):
    kept, (flipped, sems) = refs[:-2], refs[-2:]
    copies = loads(cov_ref, first, kept, sems)
    for copy in copies:
        copy.start()
    frames, atoms, slots = near_ref.shape
    lanes = frames * atoms
    whole, _ = counts_ref.shape
    flipped[...] = near_ref[...].reshape(lanes, slots).T
    chunk = min(256, whole)
    unroll = next(u for u in (6, 4, 3, 2, 1) if slots % u == 0)
    for base in range(0, whole, chunk):
        atom = lax.broadcasted_iota(jnp.int32, (chunk, lanes), 0) + base

        def step(s, total):
            for u in range(unroll):
                row = flipped[pl.ds(s * unroll + u, 1), :]
                total = jnp.where(atom == row, total + 1.0, total)
            return total

        total = lax.fori_loop(0, slots // unroll, step, jnp.zeros((chunk, lanes), F32))
        counts_ref[pl.ds(base, chunk), :] = total.astype(BF16)
    for copy in copies:
        copy.wait()


def adjoint_kernel(slots, width, *refs):
    counts_ref, kinds_ref, scale_ref, masked_ref = refs[:4]
    pieces, (out_ref, lookup) = refs[4:-2], refs[-2:]
    frames, atoms, _ = pieces[0].shape
    lanes = frames * atoms
    me = lax.axis_index("col")
    for k, piece in enumerate(pieces):
        start = pl.multiple_of((me ^ k) * atoms, atoms)
        for f in range(frames):
            lookup[f, pl.ds(start, atoms), :] = piece[f, :, pl.ds(0, width)]
    lane = lax.broadcasted_iota(jnp.int32, (1, lanes), 1)
    total = jnp.zeros((width, lanes), F32)
    for f in range(frames):
        part = lax.dot_general(
            lookup[f], counts_ref[...], (((0,), (0,)), ((), ())), preferred_element_type=F32
        )
        total = jnp.where((lane // atoms) == f, part, total)
    own = pieces[0][:, :, pl.ds(0, width)].reshape(lanes, width).astype(F32).T
    total = own + total * (1.0 / math.sqrt(slots))
    kinds = jnp.concatenate([kinds_ref[f : f + 1, :] for f in range(frames)], axis=1)
    gain = scale_ref[...].T
    scale = jnp.zeros((width, lanes), F32)
    for t in range(scale_ref.shape[0]):
        scale = jnp.where(kinds == t, gain[:, t : t + 1], scale)
    out_ref[pl.ds(0, width), :] = scale * total
    out_ref[pl.ds(width, masked_ref.shape[0]), :] = masked_ref[...]


def jacobian_kernel(count, peers, width_in, skip, span, first_row, *refs):
    sides, packs, cov_ref = refs[:count], refs[count : 2 * count], refs[2 * count]
    outs, kept = refs[2 * count + 1 : 2 * count + 1 + peers], refs[2 * count + 1 + peers : -4]
    inputs, mixed, flat, sems = refs[-4:]
    copies = loads(cov_ref, first_row, kept, sems)
    for copy in copies:
        copy.start()
    row, col = lax.axis_index("row"), lax.axis_index("col")
    frames, atoms, _ = packs[0].shape
    lanes = frames * atoms
    measures = outs[0].shape[0]
    width_out = sides[0].shape[0] - measures
    for k, pack in enumerate(packs):
        inputs[pl.ds(k * lanes, lanes), :] = pack[:, :, pl.ds(width_out, width_in)].reshape(
            lanes, width_in
        )

    def block(targets, base, held, first):
        size = min(8, held)

        def group(g, carry):
            start = first + g * size
            for k, side in enumerate(sides):
                sens = side[pl.ds(width_out, measures), :]
                for b in range(size):
                    line = side[pl.ds(start + b, 1), :]
                    mixed[pl.ds(b * measures, measures), pl.ds(k * lanes, lanes)] = (
                        sens * line
                    ).astype(BF16)
            found = jnp.dot(
                mixed[pl.ds(0, size * measures), :], inputs[...], preferred_element_type=F32
            )
            for b in range(size):
                flat[:, pl.ds(b * width_in, width_in)] = found[
                    b * measures : (b + 1) * measures, :
                ]
            reach = size * width_in
            at = base + g * reach
            if reach % 128 == 0:
                at = pl.multiple_of(at, 128)
            for target in targets:
                target[:, pl.ds(at, reach)] = flat[:, pl.ds(0, reach)].astype(BF16)
            return carry

        if held == size:
            group(0, 0)
        else:
            lax.fori_loop(0, held // size, group, 0)

    per_row = width_out // peers
    for k in range(peers):
        block([outs[k]], 0, span // width_in, (row ^ k) * per_row + skip // width_in)
    side_span = (outs[0].shape[1] - span) // width_in
    if side_span:
        block(outs, span, side_span, col * side_span)
    for copy in copies:
        copy.wait()


def multiply(whole_ref, jac, base, depth, part, tiles):
    def tile(i, carry):
        at = i * depth
        if not isinstance(i, int):
            at = pl.multiple_of(at, depth)
        left = jac[:, pl.ds(base + at, depth)]
        block = part[pl.ds(at, depth), :]
        high = block.astype(BF16)
        low = (block - high.astype(F32)).astype(BF16)
        whole_ref[...] += jnp.dot(left, high, preferred_element_type=F32) + jnp.dot(
            left, low, preferred_element_type=F32
        )
        return carry

    if tiles == 1:
        tile(0, 0)
    else:
        lax.fori_loop(0, tiles, tile, 0)


def arrange(target, sources, start, span):
    me = lax.axis_index("row")
    for k, source in enumerate(sources):
        measures = source.shape[0]
        at = pl.multiple_of((me ^ k) * measures, measures)
        target[pl.ds(at, measures), :] = source[:, pl.ds(start, span)].astype(target.dtype)


def product_first_kernel(peers, depth, *refs):
    jac_refs, kept, (whole_ref, jac) = refs[:peers], refs[peers:-2], refs[-2:]
    arrange(jac, jac_refs, 0, jac.shape[1])
    whole_ref[...] = jnp.zeros_like(whole_ref)
    base = 0
    for part in kept:
        multiply(whole_ref, jac, base, depth, part, part.shape[0] // depth)
        base += part.shape[0]


def product_last_kernel(peers, depth, count, *refs):
    jac_refs, begun_ref, kept = refs[:peers], refs[peers], refs[peers + 1 : peers + 1 + count]
    cov_ref = refs[peers + 1 + count]
    outs, (jac, side, whole, tiles, sems) = refs[peers + 2 + count : -5], refs[-5:]
    slots = tiles.shape[0]
    span = jac.shape[1]
    held = sum(part.shape[0] for part in kept)
    start = cov_ref.shape[0] - span + held
    copies = [
        pltpu.make_async_copy(
            cov_ref.at[pl.ds(start + i * depth, depth), :], tiles.at[i % slots], sems.at[i % slots]
        )
        for i in range((span - held) // depth)
    ]
    for copy in copies[:slots]:
        copy.start()
    arrange(jac, jac_refs, 0, span)
    arrange(side, jac_refs, span, side.shape[1])
    whole[...] = begun_ref[...]
    base = 0
    for part in kept:
        multiply(whole, jac, base, depth, part, part.shape[0] // depth)
        base += part.shape[0]
    for i, copy in enumerate(copies):
        copy.wait()
        multiply(whole, jac, base + i * depth, depth, tiles.at[i % slots], 1)
        if i + slots < len(copies):
            copies[i + slots].start()
    inner = lax.dot_general(
        whole[...], side[...], (((1,), (1,)), ((), ())), precision=FULL, preferred_element_type=F32
    )
    me = lax.axis_index("row")
    overall, width = whole.shape
    measures = overall // peers
    for k in range(peers):
        at = pl.multiple_of((me ^ k) * measures, measures)
        outs[k][:, pl.ds(0, width)] = whole[pl.ds(at, measures), :]
        outs[k][:, pl.ds(width, overall * peers)] = jnp.concatenate(
            [inner[q * measures : (q + 1) * measures, :] for q in range(peers)], axis=1
        )


def sum_kernel(*refs):
    parts, (exact_ref, sent_ref) = refs[:-2], refs[-2:]
    width = exact_ref.shape[1]
    total = parts[0][...]
    for part in parts[1:]:
        total = total + part[...]
    exact_ref[...] = total[:, :width]
    sent_ref[:, pl.ds(0, width)] = total[:, :width].astype(BF16)
    inner = total[:, width:]
    high = inner.astype(BF16)
    sent_ref[:, pl.ds(width, inner.shape[1])] = high
    sent_ref[:, pl.ds(width + inner.shape[1], inner.shape[1])] = (
        inner - high.astype(F32)
    ).astype(BF16)


def route_kernel(peers, width, exact_ref, *refs):
    pieces, outs, (inner_ref, held, rest) = refs[: -peers - 3], refs[-peers - 3 : -3], refs[-3:]
    row, col = lax.axis_index("row"), lax.axis_index("col")
    count = len(pieces)
    per_block = count // peers
    measures, _ = exact_ref.shape
    overall = inner_ref.shape[0]
    share = width // peers
    exact = exact_ref[...]
    low = exact - exact.astype(BF16).astype(F32)
    for q in range(peers):
        rest[q] = low[:, q * share : (q + 1) * share]
    total = jnp.zeros((measures, overall * peers), F32)
    for k, piece in enumerate(pieces):
        held[(col // 2) ^ k] = piece[:, pl.ds(0, width)]
        total = total + piece[:, pl.ds(width, overall * peers)].astype(F32)
        total = total + piece[:, pl.ds(width + overall * peers, overall * peers)].astype(F32)
    for q in range(peers):
        inner_ref[pl.ds(q * measures, measures), :] = total[:, q * overall : (q + 1) * overall]
    for k in range(peers):
        for p in range(per_block):
            outs[k][:, pl.ds(p * width, width)] = held[(row ^ k) * per_block + p]
        outs[k][:, pl.ds(per_block * width, width)] = pieces[0][:, pl.ds(0, width)]
        outs[k][:, pl.ds((per_block + 1) * width, share)] = rest[row ^ k].astype(BF16)


def inverse_kernel(*refs):
    inner_refs, (noise_ref, innovation_ref, inverse_ref, weight_ref) = refs[:2], refs[2:]
    overall = inverse_ref.shape[0]
    inner = inner_refs[0][...] + inner_refs[1][...]
    down = lax.broadcasted_iota(jnp.int32, (overall, overall), 0)
    across = lax.broadcasted_iota(jnp.int32, (overall, overall), 1)
    diagonal = down == across
    inner = inner + jnp.where(diagonal, noise_ref[...], 0.0)
    scale = 1.0 / jnp.max(jnp.sum(jnp.abs(inner), axis=1, keepdims=True), axis=0, keepdims=True)
    inverse = jnp.where(diagonal, scale, 0.0)
    for _ in range(NS_ITERS):
        left = jnp.dot(inverse, inner, precision=FULL, preferred_element_type=F32)
        inverse = 2.0 * inverse - jnp.dot(left, inverse, precision=FULL, preferred_element_type=F32)
    inverse_ref[...] = inverse
    weight_ref[...] = jnp.sum(inverse * innovation_ref[...], axis=1, keepdims=True)


def merge_kernel(weight_ref, *refs):
    pieces, (half_ref, right_ref, change_ref) = refs[:-3], refs[-3:]
    me = lax.axis_index("row")
    peers = len(pieces)
    measures = pieces[0].shape[0]
    span, width = half_ref.shape[1], right_ref.shape[1]
    share = width // peers
    total = jnp.zeros((measures, share), F32)
    for k, piece in enumerate(pieces):
        at = pl.multiple_of((me ^ k) * measures, measures)
        half_ref[pl.ds(at, measures), :] = piece[:, pl.ds(0, span)]
        right = piece[:, pl.ds(span, width)]
        right_ref[pl.ds(at, measures), :] = right
        right = right.astype(F32)
        exact = piece[:, pl.ds(span + width, share)].astype(F32)
        for q in range(peers):
            exact = exact + jnp.where(me == q, right[:, q * share : (q + 1) * share], 0.0)
        total = total + weight_ref[pl.ds(at, measures), :] * exact
    change_ref[...] = jnp.sum(total, axis=0, keepdims=True)


def update_kernel(depth, weights_ref, moved_ref, *refs):
    mine_ref, other_ref, right_ref, inverse_ref = refs[:4]
    kept, (cov_ref, weights_new_ref, out_ref) = refs[4:-11], refs[-11:-8]
    numerator, left, fresh, done, loaded, sems, fixed, fixed_sem = refs[-8:]
    height, width = cov_ref.shape
    skipped = height - fresh.shape[0]
    size = kept[0].shape[0]
    copies = loads(
        cov_ref,
        skipped,
        [fresh.at[pl.ds(at, size), :] for at in range(0, height - skipped, size)],
        loaded,
    )
    for copy in copies:
        copy.start()
    fixed[...] = weights_ref[...] + moved_ref[0, :]
    fix = pltpu.make_async_copy(fixed, weights_new_ref, fixed_sem)
    fix.start()
    core = lax.axis_index("col") % 2
    for p in range(height // (2 * width)):
        part = pl.ds(p * width, width)
        here, there = mine_ref[:, part], other_ref[:, part]
        numerator[:, pl.ds(2 * p * width, width)] = jnp.where(core == 0, here, there)
        numerator[:, pl.ds((2 * p + 1) * width, width)] = jnp.where(core == 0, there, here)
    slots = done.shape[0]

    def leave(slot, at):
        return pltpu.make_async_copy(
            done.at[slot], out_ref.at[pl.ds(at, depth), :], sems.at[slot]
        )

    parts = [(part, 0, None) for part in kept]
    parts += [(fresh, k * size, copy) for k, copy in enumerate(copies)]
    for k, (part, base, copy) in enumerate(parts):
        left[...] = lax.dot_general(
            inverse_ref[...],
            numerator[:, pl.ds(k * size, size)].astype(F32),
            (((0,), (0,)), ((), ())),
            precision=FULL,
            preferred_element_type=F32,
        ).astype(BF16)
        if copy is not None:
            copy.wait()

        def tile(i, carry, k=k, part=part, base=base):
            at = pl.multiple_of(i * depth, depth)
            gain = left[:, pl.ds(at, depth)]
            count = i + k * (size // depth)
            slot = lax.rem(count, slots)

            @pl.when(count >= slots)
            def _():
                leave(slot, 0).wait()

            for start in range(0, width, CUT):
                cut = pl.ds(start, min(CUT, width - start))
                done[slot, :, cut] = part[pl.ds(base + at, depth), cut] - lax.dot_general(
                    gain, right_ref[:, cut], (((0,), (0,)), ((), ())), preferred_element_type=F32
                )
            leave(slot, pl.multiple_of(k * size + at, depth)).start()
            return carry

        lax.fori_loop(0, size // depth, tile, 0)
    for slot in range(slots):
        leave(slot, 0).wait()
    fix.wait()


def on_device(
    cov,
    weights,
    act,
    upstream,
    neighbors,
    types,
    type_gain,
    sens,
    frame_for_measure,
    noise_variance,
    innovation,
):
    rows, cols = lax.axis_size("row"), lax.axis_size("col")
    frames, atoms, width_in = act.shape
    width_out = upstream.shape[2]
    slots = neighbors.shape[2]
    lanes = frames * atoms
    measures = sens.shape[0]
    overall = measures * rows
    height, width = cov.shape
    part = weights.shape[0]
    dma = pltpu.SemaphoreType.DMA
    depth = next(d for d in (256, 128) if height % d == 0)
    tiles = height // depth
    each = next(n for n in EACH if tiles % n == 0)
    segments = tiles // each
    held = resident((each * depth, width))
    early, later = segments * EARLY // 6, segments * LATER // 6
    packed_width = width_out + -(-width_in // 128) * 128

    packed, near, kinds, scale, masked = pl.pallas_call(
        pack_kernel,
        out_shape=[
            shape((frames, atoms, packed_width), BF16),
            shape(neighbors.shape, jnp.int32),
            shape(types.shape, jnp.int32),
            shape(type_gain.shape),
            shape((measures, lanes)),
        ],
        in_specs=[ANY] * 7,
        out_specs=[VMEM] * 5,
        scratch_shapes=[
            pltpu.VMEM(upstream.shape, BF16),
            pltpu.VMEM(act.shape, BF16),
            pltpu.VMEM(sens.shape, F32),
            pltpu.SMEM(frame_for_measure.shape, jnp.int32),
            dma((7,)),
        ],
        compiler_params=params(3),
        name="pack",
    )(*map(outside, (upstream, act, neighbors, types, type_gain, sens, frame_for_measure)))
    packs = gather(packed)
    counts, *kept = pl.pallas_call(
        functools.partial(counts_kernel, 0),
        out_shape=[shape((atoms * cols, lanes), BF16)] + [held] * early,
        in_specs=[VMEM, ANY],
        out_specs=[VMEM] * (1 + early),
        scratch_shapes=[pltpu.VMEM((slots, lanes), jnp.int32), dma((early,))],
        compiler_params=params(3),
        cost_estimate=estimate(3 * 10**9, 4 * early * each * depth * width),
        name="counts",
    )(near, outside(cov))
    side = pl.pallas_call(
        functools.partial(adjoint_kernel, slots, width_out),
        out_shape=shape((width_out + measures, lanes)),
        in_specs=[VMEM] * (4 + cols),
        out_specs=VMEM,
        scratch_shapes=[pltpu.VMEM((frames, atoms * cols, width_out), BF16)],
        compiler_params=params(3),
        name="adjoint",
    )(counts, kinds, scale, masked, *packs)
    sides = gather(side)
    part_a = tiles // 2 // each * each * depth
    part_b = height - part_a
    kept = list(kept)
    jacs = []
    for skip, size, extra, loaded in (
        (0, part_a, 0, later // 2),
        (part_a, part_b, width, later - later // 2),
    ):
        found = pl.pallas_call(
            functools.partial(
                jacobian_kernel, cols, rows, width_in, skip, size, len(kept) * each * depth
            ),
            out_shape=[shape((measures, size + extra), BF16)] * rows + [held] * loaded,
            in_specs=[VMEM] * (2 * cols) + [ANY],
            out_specs=[VMEM] * (rows + loaded),
            scratch_shapes=[
                pltpu.VMEM((cols * lanes, width_in), BF16),
                pltpu.VMEM((8 * measures, cols * lanes), BF16),
                pltpu.VMEM((measures, 8 * width_in), F32),
                dma((max(1, loaded),)),
            ],
            compiler_params=params(5),
            cost_estimate=estimate(3 * 10**9, 4 * loaded * each * depth * width),
            name="jacobian_last" if skip else "jacobian_first",
        )(*sides, *packs, outside(cov))
        kept += found[rows:]
        jacs.append(exchange(found[:rows]))
    first = part_a // (each * depth)
    begun = pl.pallas_call(
        functools.partial(product_first_kernel, rows, depth),
        out_shape=shape((overall, width)),
        in_specs=[VMEM] * (rows + first),
        out_specs=VMEM,
        scratch_shapes=[pltpu.VMEM((overall, part_a), BF16)],
        compiler_params=params(9),
        cost_estimate=estimate(8 * overall * part_a * width, 4 * part_a * width),
        name="product_first",
    )(*jacs[0], *map(keep, kept[:first]))
    rest = len(kept) - first
    parts = pl.pallas_call(
        functools.partial(product_last_kernel, rows, depth, rest),
        out_shape=[shape((measures, width + overall * rows))] * rows,
        in_specs=[VMEM] * (rows + 1 + rest) + [ANY],
        out_specs=[VMEM] * rows,
        scratch_shapes=[
            pltpu.VMEM((overall, part_b), BF16),
            pltpu.VMEM((overall, width), F32),
            pltpu.VMEM((overall, width), F32),
            pltpu.VMEM((2, depth, width), F32),
            dma((2,)),
        ],
        compiler_params=params(14),
        cost_estimate=estimate(8 * overall * part_b * width, 4 * part_b * width),
        name="product_last",
    )(*jacs[1], begun, *map(keep, kept[first:]), outside(cov))
    parts = exchange(parts)
    exact, sent = pl.pallas_call(
        sum_kernel,
        out_shape=[
            shape((measures, width)),
            shape((measures, width + 2 * overall * rows), BF16),
        ],
        in_specs=[VMEM] * rows,
        out_specs=[VMEM] * 2,
        compiler_params=params(3),
        name="sum",
    )(*parts)
    sents = gather_apart(sent)
    span = height // 2
    *routed, inner = pl.pallas_call(
        functools.partial(route_kernel, rows, width),
        out_shape=[shape((measures, span + width + part), BF16)] * rows
        + [shape((overall, overall))],
        in_specs=[VMEM] * (1 + cols // 2),
        out_specs=[VMEM] * (rows + 1),
        scratch_shapes=[
            pltpu.VMEM((cols // 2, measures, width), BF16),
            pltpu.VMEM((rows, measures, part), F32),
        ],
        compiler_params=params(3),
        name="route",
    )(exact, *sents)
    routed = exchange(routed)
    shared = swap(inner, "col", 1)
    inverse, weight = pl.pallas_call(
        inverse_kernel,
        out_shape=[shape((overall, overall)), shape((overall, 1))],
        in_specs=[VMEM] * 4,
        out_specs=[VMEM] * 2,
        compiler_params=params(3),
        name="inverse",
    )(inner, shared, noise_variance[None, :], innovation[None, :])
    half, right, change = pl.pallas_call(
        merge_kernel,
        out_shape=[
            shape((overall, span), BF16),
            shape((overall, width), BF16),
            shape((1, part)),
        ],
        in_specs=[VMEM] * (1 + rows),
        out_specs=[VMEM] * 3,
        compiler_params=params(3),
        name="merge",
    )(weight, *routed)
    other = swap(half, "col", 1)
    pairs = [(r * cols + c, c * rows + r) for r in range(rows) for c in range(cols)]
    moved = lax.ppermute(change, ("row", "col"), pairs)
    size = each * depth
    fresh = height - len(kept) * size
    weights_new, cov_new = pl.pallas_call(
        functools.partial(update_kernel, THIN),
        out_shape=[shape((part,)), shape((height, width))],
        in_specs=[VMEM] * (6 + len(kept)) + [ANY],
        out_specs=[ANY, ANY],
        scratch_shapes=[
            pltpu.VMEM((overall, height), BF16),
            pltpu.VMEM((overall, size), BF16),
            pltpu.VMEM((fresh, width), F32),
            pltpu.VMEM((SLOTS, THIN, width), F32),
            dma((fresh // size,)),
            dma((SLOTS,)),
            pltpu.VMEM((part,), F32),
            dma,
        ],
        compiler_params=params(15),
        cost_estimate=estimate(2 * overall * height * width, 4 * height * width),
        name="update",
    )(weights, moved, half, other, right, inverse, *map(keep, kept), outside(cov))
    return (weights_new, cov_new)


def solution(mesh):
    return jax.shard_map(
        on_device,
        mesh=mesh,
        in_specs=(
            P("row", "col"),
            P(("row", "col")),
            P("row", "col", None),
            P("row", "col", None),
            P("row", "col", None),
            P("row", "col"),
            P(),
            P("row", "col"),
            P("row"),
            P(),
            P(),
        ),
        out_specs=(P(("row", "col")), P("row", "col")),
        check_vma=False,
    )
```

```python
import functools
import math

import jax
import jax.numpy as jnp
from jax import lax
from jax.experimental import pallas as pl
from jax.experimental.pallas import tpu as pltpu
from jax.sharding import PartitionSpec as P


NS_ITERS = 5
FULL = lax.Precision.HIGHEST
F32 = jnp.float32
BF16 = jnp.bfloat16
EACH = (3, 2, 1)
EARLY, LATER = 3, 2
CUT = 768
THIN, SLOTS = 128, 6

VMEM = pl.BlockSpec(memory_space=pltpu.VMEM)
SMEM = pl.BlockSpec(memory_space=pltpu.SMEM)


ANY = pl.BlockSpec(memory_space=pl.ANY)


def swap(block, axis, step):
    n = lax.axis_size(axis)
    return lax.ppermute(block, axis, [(i, i ^ step) for i in range(n)])


def gather_apart(block):
    return [block] + [swap(block, "col", k) for k in range(2, lax.axis_size("col"), 2)]


def exchange(blocks):
    return [blocks[0]] + [swap(block, "row", k) for k, block in enumerate(blocks) if k]


def gather(block):
    pieces = []
    for piece in gather_apart(block):
        pieces += [piece, swap(piece, "col", 1)]
    return pieces


def params(mib):
    return pltpu.CompilerParams(vmem_limit_bytes=mib * 2**20)


def shape(dims, kind=F32):
    return jax.ShapeDtypeStruct(dims, kind)


def resident(dims, kind=F32):
    return pltpu.VMEM(dims, kind)


def outside(block):
    return pltpu.with_memory_space_constraint(block, pltpu.HBM)


def keep(block):
    return pltpu.with_memory_space_constraint(block, pltpu.VMEM)


def estimate(flops, moved):
    return pl.CostEstimate(flops=flops, bytes_accessed=moved, transcendentals=0)


def loads(source, first, targets, sems):
    copies = []
    for i, target in enumerate(targets):
        rows = target.shape[0]
        copies.append(
            pltpu.make_async_copy(source.at[pl.ds(first, rows), :], target, sems.at[i])
        )
        first += rows
    return copies


def pack_kernel(
    up_ref, act_ref, neighbors_ref, types_ref, gain_ref, sens_ref, frame_ref,
    packed_ref, near_ref, kinds_ref, scale_ref, masked_ref,
    up, act, sens, frame_of, sems,
):
    copies = [
        pltpu.make_async_copy(source, target, sems.at[i])
        for i, (source, target) in enumerate(
            (
                (up_ref, up),
                (act_ref, act),
                (neighbors_ref, near_ref),
                (types_ref, kinds_ref),
                (gain_ref, scale_ref),
                (sens_ref, sens),
                (frame_ref, frame_of),
            )
        )
    ]
    for copy in copies:
        copy.start()
    for copy in copies:
        copy.wait()
    width_out, width_in = up.shape[2], act.shape[2]
    packed_ref[:, :, pl.ds(0, width_out)] = up[...]
    packed_ref[:, :, pl.ds(width_out, width_in)] = act[...]
    measures, _ = sens.shape
    frames = up.shape[0]
    index = lax.broadcasted_iota(jnp.int32, sens.shape, 0)
    frame = jnp.zeros(sens.shape, jnp.int32)
    for m in range(measures):
        frame = jnp.where(index == m, frame_of[m], frame)
    masked_ref[...] = jnp.concatenate(
        [jnp.where(frame == f, sens[...], 0.0) for f in range(frames)], axis=1
    )


def counts_kernel(first, near_ref, cov_ref, counts_ref, *refs):
    kept, (flipped, sems) = refs[:-2], refs[-2:]
    copies = loads(cov_ref, first, kept, sems)
    for copy in copies:
        copy.start()
    frames, atoms, slots = near_ref.shape
    lanes = frames * atoms
    whole, _ = counts_ref.shape
    flipped[...] = near_ref[...].reshape(lanes, slots).T
    chunk = min(256, whole)
    unroll = next(u for u in (6, 4, 3, 2, 1) if slots % u == 0)
    for base in range(0, whole, chunk):
        atom = lax.broadcasted_iota(jnp.int32, (chunk, lanes), 0) + base

        def step(s, total):
            for u in range(unroll):
                row = flipped[pl.ds(s * unroll + u, 1), :]
                total = jnp.where(atom == row, total + 1.0, total)
            return total

        total = lax.fori_loop(0, slots // unroll, step, jnp.zeros((chunk, lanes), F32))
        counts_ref[pl.ds(base, chunk), :] = total.astype(BF16)
    for copy in copies:
        copy.wait()


def adjoint_kernel(slots, width, *refs):
    counts_ref, kinds_ref, scale_ref, masked_ref = refs[:4]
    pieces, (out_ref, lookup) = refs[4:-2], refs[-2:]
    frames, atoms, _ = pieces[0].shape
    lanes = frames * atoms
    me = lax.axis_index("col")
    for k, piece in enumerate(pieces):
        start = pl.multiple_of((me ^ k) * atoms, atoms)
        for f in range(frames):
            lookup[f, pl.ds(start, atoms), :] = piece[f, :, pl.ds(0, width)]
    lane = lax.broadcasted_iota(jnp.int32, (1, lanes), 1)
    total = jnp.zeros((width, lanes), F32)
    for f in range(frames):
        part = lax.dot_general(
            lookup[f], counts_ref[...], (((0,), (0,)), ((), ())), preferred_element_type=F32
        )
        total = jnp.where((lane // atoms) == f, part, total)
    own = pieces[0][:, :, pl.ds(0, width)].reshape(lanes, width).astype(F32).T
    total = own + total * (1.0 / math.sqrt(slots))
    kinds = jnp.concatenate([kinds_ref[f : f + 1, :] for f in range(frames)], axis=1)
    gain = scale_ref[...].T
    scale = jnp.zeros((width, lanes), F32)
    for t in range(scale_ref.shape[0]):
        scale = jnp.where(kinds == t, gain[:, t : t + 1], scale)
    out_ref[pl.ds(0, width), :] = scale * total
    out_ref[pl.ds(width, masked_ref.shape[0]), :] = masked_ref[...]


def jacobian_kernel(count, peers, width_in, skip, span, first_row, *refs):
    sides, packs, cov_ref = refs[:count], refs[count : 2 * count], refs[2 * count]
    outs, kept = refs[2 * count + 1 : 2 * count + 1 + peers], refs[2 * count + 1 + peers : -4]
    inputs, mixed, flat, sems = refs[-4:]
    copies = loads(cov_ref, first_row, kept, sems)
    for copy in copies:
        copy.start()
    row, col = lax.axis_index("row"), lax.axis_index("col")
    frames, atoms, _ = packs[0].shape
    lanes = frames * atoms
    measures = outs[0].shape[0]
    width_out = sides[0].shape[0] - measures
    for k, pack in enumerate(packs):
        inputs[pl.ds(k * lanes, lanes), :] = pack[:, :, pl.ds(width_out, width_in)].reshape(
            lanes, width_in
        )

    def block(targets, base, held, first):
        size = min(8, held)

        def group(g, carry):
            start = first + g * size
            for k, side in enumerate(sides):
                sens = side[pl.ds(width_out, measures), :]
                for b in range(size):
                    line = side[pl.ds(start + b, 1), :]
                    mixed[pl.ds(b * measures, measures), pl.ds(k * lanes, lanes)] = (
                        sens * line
                    ).astype(BF16)
            found = jnp.dot(
                mixed[pl.ds(0, size * measures), :], inputs[...], preferred_element_type=F32
            )
            for b in range(size):
                flat[:, pl.ds(b * width_in, width_in)] = found[
                    b * measures : (b + 1) * measures, :
                ]
            reach = size * width_in
            at = base + g * reach
            if reach % 128 == 0:
                at = pl.multiple_of(at, 128)
            for target in targets:
                target[:, pl.ds(at, reach)] = flat[:, pl.ds(0, reach)].astype(BF16)
            return carry

        if held == size:
            group(0, 0)
        else:
            lax.fori_loop(0, held // size, group, 0)

    per_row = width_out // peers
    for k in range(peers):
        block([outs[k]], 0, span // width_in, (row ^ k) * per_row + skip // width_in)
    side_span = (outs[0].shape[1] - span) // width_in
    if side_span:
        block(outs, span, side_span, col * side_span)
    for copy in copies:
        copy.wait()


def multiply(whole_ref, jac, base, depth, part, tiles):
    def tile(i, carry):
        at = i * depth
        if not isinstance(i, int):
            at = pl.multiple_of(at, depth)
        left = jac[:, pl.ds(base + at, depth)]
        block = part[pl.ds(at, depth), :]
        high = block.astype(BF16)
        low = (block - high.astype(F32)).astype(BF16)
        whole_ref[...] += jnp.dot(left, high, preferred_element_type=F32) + jnp.dot(
            left, low, preferred_element_type=F32
        )
        return carry

    if tiles == 1:
        tile(0, 0)
    else:
        lax.fori_loop(0, tiles, tile, 0)


def arrange(target, sources, start, span):
    me = lax.axis_index("row")
    for k, source in enumerate(sources):
        measures = source.shape[0]
        at = pl.multiple_of((me ^ k) * measures, measures)
        target[pl.ds(at, measures), :] = source[:, pl.ds(start, span)].astype(target.dtype)


def product_first_kernel(peers, depth, *refs):
    jac_refs, kept, (whole_ref, jac) = refs[:peers], refs[peers:-2], refs[-2:]
    arrange(jac, jac_refs, 0, jac.shape[1])
    whole_ref[...] = jnp.zeros_like(whole_ref)
    base = 0
    for part in kept:
        multiply(whole_ref, jac, base, depth, part, part.shape[0] // depth)
        base += part.shape[0]


def product_last_kernel(peers, depth, count, *refs):
    jac_refs, begun_ref, kept = refs[:peers], refs[peers], refs[peers + 1 : peers + 1 + count]
    cov_ref = refs[peers + 1 + count]
    outs, (jac, side, whole, tiles, sems) = refs[peers + 2 + count : -5], refs[-5:]
    slots = tiles.shape[0]
    span = jac.shape[1]
    held = sum(part.shape[0] for part in kept)
    start = cov_ref.shape[0] - span + held
    copies = [
        pltpu.make_async_copy(
            cov_ref.at[pl.ds(start + i * depth, depth), :], tiles.at[i % slots], sems.at[i % slots]
        )
        for i in range((span - held) // depth)
    ]
    for copy in copies[:slots]:
        copy.start()
    arrange(jac, jac_refs, 0, span)
    arrange(side, jac_refs, span, side.shape[1])
    whole[...] = begun_ref[...]
    base = 0
    for part in kept:
        multiply(whole, jac, base, depth, part, part.shape[0] // depth)
        base += part.shape[0]
    for i, copy in enumerate(copies):
        copy.wait()
        multiply(whole, jac, base + i * depth, depth, tiles.at[i % slots], 1)
        if i + slots < len(copies):
            copies[i + slots].start()
    inner = lax.dot_general(
        whole[...], side[...], (((1,), (1,)), ((), ())), precision=FULL, preferred_element_type=F32
    )
    me = lax.axis_index("row")
    overall, width = whole.shape
    measures = overall // peers
    for k in range(peers):
        at = pl.multiple_of((me ^ k) * measures, measures)
        outs[k][:, pl.ds(0, width)] = whole[pl.ds(at, measures), :]
        outs[k][:, pl.ds(width, overall * peers)] = jnp.concatenate(
            [inner[q * measures : (q + 1) * measures, :] for q in range(peers)], axis=1
        )


def sum_kernel(peers, *refs):
    parts, sent_ref, outs, rest = refs[:peers], refs[peers], refs[peers + 1 : -1], refs[-1]
    row = lax.axis_index("row")
    share = rest.shape[2]
    width = share * peers
    total = parts[0][...]
    for part in parts[1:]:
        total = total + part[...]
    exact = total[:, :width]
    right = exact.astype(BF16)
    low = exact - right.astype(F32)
    for q in range(peers):
        rest[q] = low[:, q * share : (q + 1) * share]
    sent_ref[:, pl.ds(0, width)] = right
    inner = total[:, width:]
    high = inner.astype(BF16)
    sent_ref[:, pl.ds(width, inner.shape[1])] = high
    sent_ref[:, pl.ds(width + inner.shape[1], inner.shape[1])] = (
        inner - high.astype(F32)
    ).astype(BF16)
    for k, out in enumerate(outs):
        out[:, pl.ds(0, width)] = right
        out[:, pl.ds(width, share)] = rest[row ^ k].astype(BF16)


def route_kernel(peers, width, *refs):
    pieces, outs, inner_ref, held = refs[: -peers - 2], refs[-peers - 2 : -2], refs[-2], refs[-1]
    row, col = lax.axis_index("row"), lax.axis_index("col")
    count = len(pieces)
    per_block = count // peers
    measures = pieces[0].shape[0]
    overall = inner_ref.shape[0]
    total = jnp.zeros((measures, overall * peers), F32)
    for k, piece in enumerate(pieces):
        held[(col // 2) ^ k] = piece[:, pl.ds(0, width)]
        total = total + piece[:, pl.ds(width, overall * peers)].astype(F32)
        total = total + piece[:, pl.ds(width + overall * peers, overall * peers)].astype(F32)
    for q in range(peers):
        inner_ref[pl.ds(q * measures, measures), :] = total[:, q * overall : (q + 1) * overall]
    for k in range(peers):
        for p in range(per_block):
            outs[k][:, pl.ds(p * width, width)] = held[(row ^ k) * per_block + p]


def inverse_kernel(*refs):
    inner_refs, (noise_ref, innovation_ref, inverse_ref, weight_ref) = refs[:2], refs[2:]
    overall = inverse_ref.shape[0]
    inner = inner_refs[0][...] + inner_refs[1][...]
    down = lax.broadcasted_iota(jnp.int32, (overall, overall), 0)
    across = lax.broadcasted_iota(jnp.int32, (overall, overall), 1)
    diagonal = down == across
    inner = inner + jnp.where(diagonal, noise_ref[...], 0.0)
    scale = 1.0 / jnp.max(jnp.sum(jnp.abs(inner), axis=1, keepdims=True), axis=0, keepdims=True)
    inverse = jnp.where(diagonal, scale, 0.0)
    for _ in range(NS_ITERS):
        left = jnp.dot(inverse, inner, precision=FULL, preferred_element_type=F32)
        inverse = 2.0 * inverse - jnp.dot(left, inverse, precision=FULL, preferred_element_type=F32)
    inverse_ref[...] = inverse
    weight_ref[...] = jnp.sum(inverse * innovation_ref[...], axis=1, keepdims=True)


def merge_kernel(peers, weight_ref, *refs):
    pieces, blocks = refs[:peers], refs[peers : 2 * peers]
    half_ref, right_ref, change_ref = refs[2 * peers :]
    me = lax.axis_index("row")
    width = right_ref.shape[1]
    share = width // peers
    measures = pieces[0].shape[0]
    arrange(half_ref, pieces, 0, half_ref.shape[1])
    arrange(right_ref, blocks, 0, width)
    total = jnp.zeros((measures, share), F32)
    for k, block in enumerate(blocks):
        at = pl.multiple_of((me ^ k) * measures, measures)
        right = block[:, pl.ds(0, width)].astype(F32)
        exact = block[:, pl.ds(width, share)].astype(F32)
        for q in range(peers):
            exact = exact + jnp.where(me == q, right[:, q * share : (q + 1) * share], 0.0)
        total = total + weight_ref[pl.ds(at, measures), :] * exact
    change_ref[...] = jnp.sum(total, axis=0, keepdims=True)


def update_kernel(depth, weights_ref, moved_ref, *refs):
    mine_ref, other_ref, right_ref, inverse_ref = refs[:4]
    kept, (cov_ref, weights_new_ref, out_ref) = refs[4:-11], refs[-11:-8]
    numerator, left, fresh, done, loaded, sems, fixed, fixed_sem = refs[-8:]
    height, width = cov_ref.shape
    skipped = height - fresh.shape[0]
    size = kept[0].shape[0]
    copies = loads(
        cov_ref,
        skipped,
        [fresh.at[pl.ds(at, size), :] for at in range(0, height - skipped, size)],
        loaded,
    )
    for copy in copies:
        copy.start()
    fixed[...] = weights_ref[...] + moved_ref[0, :]
    fix = pltpu.make_async_copy(fixed, weights_new_ref, fixed_sem)
    fix.start()
    core = lax.axis_index("col") % 2
    for p in range(height // (2 * width)):
        part = pl.ds(p * width, width)
        here, there = mine_ref[:, part], other_ref[:, part]
        numerator[:, pl.ds(2 * p * width, width)] = jnp.where(core == 0, here, there)
        numerator[:, pl.ds((2 * p + 1) * width, width)] = jnp.where(core == 0, there, here)
    slots = done.shape[0]

    def leave(slot, at):
        return pltpu.make_async_copy(
            done.at[slot], out_ref.at[pl.ds(at, depth), :], sems.at[slot]
        )

    parts = [(part, 0, None) for part in kept]
    parts += [(fresh, k * size, copy) for k, copy in enumerate(copies)]
    for k, (part, base, copy) in enumerate(parts):
        left[...] = lax.dot_general(
            inverse_ref[...],
            numerator[:, pl.ds(k * size, size)].astype(F32),
            (((0,), (0,)), ((), ())),
            precision=FULL,
            preferred_element_type=F32,
        ).astype(BF16)
        if copy is not None:
            copy.wait()

        def tile(i, carry, k=k, part=part, base=base):
            at = pl.multiple_of(i * depth, depth)
            gain = left[:, pl.ds(at, depth)]
            count = i + k * (size // depth)
            slot = lax.rem(count, slots)

            @pl.when(count >= slots)
            def _():
                leave(slot, 0).wait()

            for start in range(0, width, CUT):
                cut = pl.ds(start, min(CUT, width - start))
                done[slot, :, cut] = part[pl.ds(base + at, depth), cut] - lax.dot_general(
                    gain, right_ref[:, cut], (((0,), (0,)), ((), ())), preferred_element_type=F32
                )
            leave(slot, pl.multiple_of(k * size + at, depth)).start()
            return carry

        lax.fori_loop(0, size // depth, tile, 0)
    for slot in range(slots):
        leave(slot, 0).wait()
    fix.wait()


def on_device(
    cov,
    weights,
    act,
    upstream,
    neighbors,
    types,
    type_gain,
    sens,
    frame_for_measure,
    noise_variance,
    innovation,
):
    rows, cols = lax.axis_size("row"), lax.axis_size("col")
    frames, atoms, width_in = act.shape
    width_out = upstream.shape[2]
    slots = neighbors.shape[2]
    lanes = frames * atoms
    measures = sens.shape[0]
    overall = measures * rows
    height, width = cov.shape
    part = weights.shape[0]
    dma = pltpu.SemaphoreType.DMA
    depth = next(d for d in (256, 128) if height % d == 0)
    tiles = height // depth
    each = next(n for n in EACH if tiles % n == 0)
    segments = tiles // each
    held = resident((each * depth, width))
    early, later = segments * EARLY // 6, segments * LATER // 6
    packed_width = width_out + -(-width_in // 128) * 128

    packed, near, kinds, scale, masked = pl.pallas_call(
        pack_kernel,
        out_shape=[
            shape((frames, atoms, packed_width), BF16),
            shape(neighbors.shape, jnp.int32),
            shape(types.shape, jnp.int32),
            shape(type_gain.shape),
            shape((measures, lanes)),
        ],
        in_specs=[ANY] * 7,
        out_specs=[VMEM] * 5,
        scratch_shapes=[
            pltpu.VMEM(upstream.shape, BF16),
            pltpu.VMEM(act.shape, BF16),
            pltpu.VMEM(sens.shape, F32),
            pltpu.SMEM(frame_for_measure.shape, jnp.int32),
            dma((7,)),
        ],
        compiler_params=params(3),
        name="pack",
    )(*map(outside, (upstream, act, neighbors, types, type_gain, sens, frame_for_measure)))
    packs = gather(packed)
    counts, *kept = pl.pallas_call(
        functools.partial(counts_kernel, 0),
        out_shape=[shape((atoms * cols, lanes), BF16)] + [held] * early,
        in_specs=[VMEM, ANY],
        out_specs=[VMEM] * (1 + early),
        scratch_shapes=[pltpu.VMEM((slots, lanes), jnp.int32), dma((early,))],
        compiler_params=params(3),
        cost_estimate=estimate(3 * 10**9, 4 * early * each * depth * width),
        name="counts",
    )(near, outside(cov))
    side = pl.pallas_call(
        functools.partial(adjoint_kernel, slots, width_out),
        out_shape=shape((width_out + measures, lanes)),
        in_specs=[VMEM] * (4 + cols),
        out_specs=VMEM,
        scratch_shapes=[pltpu.VMEM((frames, atoms * cols, width_out), BF16)],
        compiler_params=params(3),
        name="adjoint",
    )(counts, kinds, scale, masked, *packs)
    sides = gather(side)
    part_a = tiles // 2 // each * each * depth
    part_b = height - part_a
    kept = list(kept)
    jacs = []
    for skip, size, extra, loaded in (
        (0, part_a, 0, later // 2),
        (part_a, part_b, width, later - later // 2),
    ):
        found = pl.pallas_call(
            functools.partial(
                jacobian_kernel, cols, rows, width_in, skip, size, len(kept) * each * depth
            ),
            out_shape=[shape((measures, size + extra), BF16)] * rows + [held] * loaded,
            in_specs=[VMEM] * (2 * cols) + [ANY],
            out_specs=[VMEM] * (rows + loaded),
            scratch_shapes=[
                pltpu.VMEM((cols * lanes, width_in), BF16),
                pltpu.VMEM((8 * measures, cols * lanes), BF16),
                pltpu.VMEM((measures, 8 * width_in), F32),
                dma((max(1, loaded),)),
            ],
            compiler_params=params(5),
            cost_estimate=estimate(3 * 10**9, 4 * loaded * each * depth * width),
            name="jacobian_last" if skip else "jacobian_first",
        )(*sides, *packs, outside(cov))
        kept += found[rows:]
        jacs.append(exchange(found[:rows]))
    first = part_a // (each * depth)
    begun = pl.pallas_call(
        functools.partial(product_first_kernel, rows, depth),
        out_shape=shape((overall, width)),
        in_specs=[VMEM] * (rows + first),
        out_specs=VMEM,
        scratch_shapes=[pltpu.VMEM((overall, part_a), BF16)],
        compiler_params=params(9),
        cost_estimate=estimate(8 * overall * part_a * width, 4 * part_a * width),
        name="product_first",
    )(*jacs[0], *map(keep, kept[:first]))
    rest = len(kept) - first
    parts = pl.pallas_call(
        functools.partial(product_last_kernel, rows, depth, rest),
        out_shape=[shape((measures, width + overall * rows))] * rows,
        in_specs=[VMEM] * (rows + 1 + rest) + [ANY],
        out_specs=[VMEM] * rows,
        scratch_shapes=[
            pltpu.VMEM((overall, part_b), BF16),
            pltpu.VMEM((overall, width), F32),
            pltpu.VMEM((overall, width), F32),
            pltpu.VMEM((2, depth, width), F32),
            dma((2,)),
        ],
        compiler_params=params(14),
        cost_estimate=estimate(8 * overall * part_b * width, 4 * part_b * width),
        name="product_last",
    )(*jacs[1], begun, *map(keep, kept[first:]), outside(cov))
    parts = exchange(parts)
    sent, *blocks = pl.pallas_call(
        functools.partial(sum_kernel, rows),
        out_shape=[shape((measures, width + 2 * overall * rows), BF16)]
        + [shape((measures, width + part), BF16)] * rows,
        in_specs=[VMEM] * rows,
        out_specs=[VMEM] * (rows + 1),
        scratch_shapes=[pltpu.VMEM((rows, measures, part), F32)],
        compiler_params=params(3),
        name="sum",
    )(*parts)
    sents = gather_apart(sent)
    blocks = exchange(blocks)
    span = height // 2
    *routed, inner = pl.pallas_call(
        functools.partial(route_kernel, rows, width),
        out_shape=[shape((measures, span), BF16)] * rows + [shape((overall, overall))],
        in_specs=[VMEM] * (cols // 2),
        out_specs=[VMEM] * (rows + 1),
        scratch_shapes=[pltpu.VMEM((cols // 2, measures, width), BF16)],
        compiler_params=params(3),
        name="route",
    )(*sents)
    routed = exchange(routed)
    shared = swap(inner, "col", 1)
    inverse, weight = pl.pallas_call(
        inverse_kernel,
        out_shape=[shape((overall, overall)), shape((overall, 1))],
        in_specs=[VMEM] * 4,
        out_specs=[VMEM] * 2,
        compiler_params=params(3),
        name="inverse",
    )(inner, shared, noise_variance[None, :], innovation[None, :])
    half, right, change = pl.pallas_call(
        functools.partial(merge_kernel, rows),
        out_shape=[
            shape((overall, span), BF16),
            shape((overall, width), BF16),
            shape((1, part)),
        ],
        in_specs=[VMEM] * (1 + 2 * rows),
        out_specs=[VMEM] * 3,
        compiler_params=params(3),
        name="merge",
    )(weight, *routed, *blocks)
    other = swap(half, "col", 1)
    pairs = [(r * cols + c, c * rows + r) for r in range(rows) for c in range(cols)]
    moved = lax.ppermute(change, ("row", "col"), pairs)
    size = each * depth
    fresh = height - len(kept) * size
    weights_new, cov_new = pl.pallas_call(
        functools.partial(update_kernel, THIN),
        out_shape=[shape((part,)), shape((height, width))],
        in_specs=[VMEM] * (6 + len(kept)) + [ANY],
        out_specs=[ANY, ANY],
        scratch_shapes=[
            pltpu.VMEM((overall, height), BF16),
            pltpu.VMEM((overall, size), BF16),
            pltpu.VMEM((fresh, width), F32),
            pltpu.VMEM((SLOTS, THIN, width), F32),
            dma((fresh // size,)),
            dma((SLOTS,)),
            pltpu.VMEM((part,), F32),
            dma,
        ],
        compiler_params=params(15),
        cost_estimate=estimate(2 * overall * height * width, 4 * height * width),
        name="update",
    )(weights, moved, half, other, right, inverse, *map(keep, kept), outside(cov))
    return (weights_new, cov_new)


def solution(mesh):
    return jax.shard_map(
        on_device,
        mesh=mesh,
        in_specs=(
            P("row", "col"),
            P(("row", "col")),
            P("row", "col", None),
            P("row", "col", None),
            P("row", "col", None),
            P("row", "col"),
            P(),
            P("row", "col"),
            P("row"),
            P(),
            P(),
        ),
        out_specs=(P(("row", "col")), P("row", "col")),
        check_vma=False,
    )
```

```python
import functools
import math

import jax
import jax.numpy as jnp
from jax import lax
from jax.experimental import pallas as pl
from jax.experimental.pallas import tpu as pltpu
from jax.sharding import PartitionSpec as P


NS_ITERS = 5
FULL = lax.Precision.HIGHEST
F32 = jnp.float32
BF16 = jnp.bfloat16
EACH = (3, 2, 1)
EARLY, LATER = 3, 2
CUT = 768
THIN, SLOTS = 128, 6

VMEM = pl.BlockSpec(memory_space=pltpu.VMEM)
SMEM = pl.BlockSpec(memory_space=pltpu.SMEM)


ANY = pl.BlockSpec(memory_space=pl.ANY)


def swap(block, axis, step):
    n = lax.axis_size(axis)
    return lax.ppermute(block, axis, [(i, i ^ step) for i in range(n)])


def gather_apart(block):
    return [block] + [swap(block, "col", k) for k in range(2, lax.axis_size("col"), 2)]


def exchange(blocks):
    return [blocks[0]] + [swap(block, "row", k) for k, block in enumerate(blocks) if k]


def gather(block):
    pieces = []
    for piece in gather_apart(block):
        pieces += [piece, swap(piece, "col", 1)]
    return pieces


def params(mib):
    return pltpu.CompilerParams(vmem_limit_bytes=mib * 2**20)


def shape(dims, kind=F32):
    return jax.ShapeDtypeStruct(dims, kind)


def resident(dims, kind=F32):
    return pltpu.VMEM(dims, kind)


def outside(block):
    return pltpu.with_memory_space_constraint(block, pltpu.HBM)


def keep(block):
    return pltpu.with_memory_space_constraint(block, pltpu.VMEM)


def estimate(flops, moved):
    return pl.CostEstimate(flops=flops, bytes_accessed=moved, transcendentals=0)


def loads(source, first, targets, sems):
    copies = []
    for i, target in enumerate(targets):
        rows = target.shape[0]
        copies.append(
            pltpu.make_async_copy(source.at[pl.ds(first, rows), :], target, sems.at[i])
        )
        first += rows
    return copies


def pack_kernel(
    up_ref, act_ref, neighbors_ref, types_ref, gain_ref, sens_ref, frame_ref,
    packed_ref, near_ref, kinds_ref, scale_ref, masked_ref,
    up, act, sens, frame_of, sems,
):
    copies = [
        pltpu.make_async_copy(source, target, sems.at[i])
        for i, (source, target) in enumerate(
            (
                (up_ref, up),
                (act_ref, act),
                (neighbors_ref, near_ref),
                (types_ref, kinds_ref),
                (gain_ref, scale_ref),
                (sens_ref, sens),
                (frame_ref, frame_of),
            )
        )
    ]
    for copy in copies:
        copy.start()
    for copy in copies:
        copy.wait()
    width_out, width_in = up.shape[2], act.shape[2]
    packed_ref[:, :, pl.ds(0, width_out)] = up[...]
    packed_ref[:, :, pl.ds(width_out, width_in)] = act[...]
    measures, _ = sens.shape
    frames = up.shape[0]
    index = lax.broadcasted_iota(jnp.int32, sens.shape, 0)
    frame = jnp.zeros(sens.shape, jnp.int32)
    for m in range(measures):
        frame = jnp.where(index == m, frame_of[m], frame)
    masked_ref[...] = jnp.concatenate(
        [jnp.where(frame == f, sens[...], 0.0) for f in range(frames)], axis=1
    )


def counts_kernel(first, near_ref, cov_ref, counts_ref, *refs):
    kept, (flipped, sems) = refs[:-2], refs[-2:]
    copies = loads(cov_ref, first, kept, sems)
    for copy in copies:
        copy.start()
    frames, atoms, slots = near_ref.shape
    lanes = frames * atoms
    whole, _ = counts_ref.shape
    flipped[...] = near_ref[...].reshape(lanes, slots).T
    chunk = min(256, whole)
    unroll = next(u for u in (6, 4, 3, 2, 1) if slots % u == 0)
    for base in range(0, whole, chunk):
        atom = lax.broadcasted_iota(jnp.int32, (chunk, lanes), 0) + base

        def step(s, total):
            for u in range(unroll):
                row = flipped[pl.ds(s * unroll + u, 1), :]
                total = jnp.where(atom == row, total + 1.0, total)
            return total

        total = lax.fori_loop(0, slots // unroll, step, jnp.zeros((chunk, lanes), F32))
        counts_ref[pl.ds(base, chunk), :] = total.astype(BF16)
    for copy in copies:
        copy.wait()


def adjoint_kernel(slots, width, *refs):
    counts_ref, kinds_ref, scale_ref, masked_ref = refs[:4]
    pieces, (out_ref, lookup) = refs[4:-2], refs[-2:]
    frames, atoms, _ = pieces[0].shape
    lanes = frames * atoms
    me = lax.axis_index("col")
    for k, piece in enumerate(pieces):
        start = pl.multiple_of((me ^ k) * atoms, atoms)
        for f in range(frames):
            lookup[f, pl.ds(start, atoms), :] = piece[f, :, pl.ds(0, width)]
    lane = lax.broadcasted_iota(jnp.int32, (1, lanes), 1)
    total = jnp.zeros((width, lanes), F32)
    for f in range(frames):
        part = lax.dot_general(
            lookup[f], counts_ref[...], (((0,), (0,)), ((), ())), preferred_element_type=F32
        )
        total = jnp.where((lane // atoms) == f, part, total)
    own = pieces[0][:, :, pl.ds(0, width)].reshape(lanes, width).astype(F32).T
    total = own + total * (1.0 / math.sqrt(slots))
    kinds = jnp.concatenate([kinds_ref[f : f + 1, :] for f in range(frames)], axis=1)
    gain = scale_ref[...].T
    scale = jnp.zeros((width, lanes), F32)
    for t in range(scale_ref.shape[0]):
        scale = jnp.where(kinds == t, gain[:, t : t + 1], scale)
    out_ref[pl.ds(0, width), :] = scale * total
    out_ref[pl.ds(width, masked_ref.shape[0]), :] = masked_ref[...]


def jacobian_kernel(count, peers, width_in, skip, span, first_row, *refs):
    sides, packs, cov_ref = refs[:count], refs[count : 2 * count], refs[2 * count]
    outs, kept = refs[2 * count + 1 : 2 * count + 1 + peers], refs[2 * count + 1 + peers : -4]
    inputs, mixed, flat, sems = refs[-4:]
    copies = loads(cov_ref, first_row, kept, sems)
    for copy in copies:
        copy.start()
    row, col = lax.axis_index("row"), lax.axis_index("col")
    frames, atoms, _ = packs[0].shape
    lanes = frames * atoms
    measures = outs[0].shape[0]
    width_out = sides[0].shape[0] - measures
    for k, pack in enumerate(packs):
        inputs[pl.ds(k * lanes, lanes), :] = pack[:, :, pl.ds(width_out, width_in)].reshape(
            lanes, width_in
        )

    def block(targets, base, held, first):
        size = min(8, held)

        def group(g, carry):
            start = first + g * size
            for k, side in enumerate(sides):
                sens = side[pl.ds(width_out, measures), :]
                for b in range(size):
                    line = side[pl.ds(start + b, 1), :]
                    mixed[pl.ds(b * measures, measures), pl.ds(k * lanes, lanes)] = (
                        sens * line
                    ).astype(BF16)
            found = jnp.dot(
                mixed[pl.ds(0, size * measures), :], inputs[...], preferred_element_type=F32
            )
            for b in range(size):
                flat[:, pl.ds(b * width_in, width_in)] = found[
                    b * measures : (b + 1) * measures, :
                ]
            reach = size * width_in
            at = base + g * reach
            if reach % 128 == 0:
                at = pl.multiple_of(at, 128)
            for target in targets:
                target[:, pl.ds(at, reach)] = flat[:, pl.ds(0, reach)].astype(BF16)
            return carry

        if held == size:
            group(0, 0)
        else:
            lax.fori_loop(0, held // size, group, 0)

    per_row = width_out // peers
    for k in range(peers):
        block([outs[k]], 0, span // width_in, (row ^ k) * per_row + skip // width_in)
    side_span = (outs[0].shape[1] - span) // width_in
    if side_span:
        block(outs, span, side_span, col * side_span)
    for copy in copies:
        copy.wait()


def multiply(whole_ref, jac, base, depth, part, tiles):
    def tile(i, carry):
        at = i * depth
        if not isinstance(i, int):
            at = pl.multiple_of(at, depth)
        left = jac[:, pl.ds(base + at, depth)]
        block = part[pl.ds(at, depth), :]
        high = block.astype(BF16)
        low = (block - high.astype(F32)).astype(BF16)
        whole_ref[...] += jnp.dot(left, high, preferred_element_type=F32) + jnp.dot(
            left, low, preferred_element_type=F32
        )
        return carry

    if tiles == 1:
        tile(0, 0)
    else:
        lax.fori_loop(0, tiles, tile, 0)


def arrange(target, sources, start, span):
    me = lax.axis_index("row")
    for k, source in enumerate(sources):
        measures = source.shape[0]
        at = pl.multiple_of((me ^ k) * measures, measures)
        target[pl.ds(at, measures), :] = source[:, pl.ds(start, span)].astype(target.dtype)


def product_first_kernel(peers, depth, *refs):
    jac_refs, kept, (whole_ref, jac) = refs[:peers], refs[peers:-2], refs[-2:]
    arrange(jac, jac_refs, 0, jac.shape[1])
    whole_ref[...] = jnp.zeros_like(whole_ref)
    base = 0
    for part in kept:
        multiply(whole_ref, jac, base, depth, part, part.shape[0] // depth)
        base += part.shape[0]


def product_last_kernel(peers, depth, count, *refs):
    jac_refs, begun_ref, kept = refs[:peers], refs[peers], refs[peers + 1 : peers + 1 + count]
    cov_ref = refs[peers + 1 + count]
    outs, (jac, side, whole, tiles, sems) = refs[peers + 2 + count : -5], refs[-5:]
    slots = tiles.shape[0]
    span = jac.shape[1]
    held = sum(part.shape[0] for part in kept)
    start = cov_ref.shape[0] - span + held
    copies = [
        pltpu.make_async_copy(
            cov_ref.at[pl.ds(start + i * depth, depth), :], tiles.at[i % slots], sems.at[i % slots]
        )
        for i in range((span - held) // depth)
    ]
    for copy in copies[:slots]:
        copy.start()
    arrange(jac, jac_refs, 0, span)
    arrange(side, jac_refs, span, side.shape[1])
    whole[...] = begun_ref[...]
    base = 0
    for part in kept:
        multiply(whole, jac, base, depth, part, part.shape[0] // depth)
        base += part.shape[0]
    for i, copy in enumerate(copies):
        copy.wait()
        multiply(whole, jac, base + i * depth, depth, tiles.at[i % slots], 1)
        if i + slots < len(copies):
            copies[i + slots].start()
    inner = 0.0
    left = whole[...]
    for _ in range(3):
        term = left.astype(BF16)
        left = left - term.astype(F32)
        inner = inner + lax.dot_general(
            term, side[...], (((1,), (1,)), ((), ())), preferred_element_type=F32
        )
    me = lax.axis_index("row")
    overall, width = whole.shape
    measures = overall // peers
    for k in range(peers):
        at = pl.multiple_of((me ^ k) * measures, measures)
        outs[k][:, pl.ds(0, width)] = whole[pl.ds(at, measures), :]
        outs[k][:, pl.ds(width, overall * peers)] = jnp.concatenate(
            [inner[q * measures : (q + 1) * measures, :] for q in range(peers)], axis=1
        )


def sum_kernel(peers, *refs):
    parts, sent_ref, outs, rest = refs[:peers], refs[peers], refs[peers + 1 : -1], refs[-1]
    row = lax.axis_index("row")
    share = rest.shape[2]
    width = share * peers
    total = parts[0][...]
    for part in parts[1:]:
        total = total + part[...]
    exact = total[:, :width]
    right = exact.astype(BF16)
    low = exact - right.astype(F32)
    for q in range(peers):
        rest[q] = low[:, q * share : (q + 1) * share]
    sent_ref[:, pl.ds(0, width)] = right
    inner = total[:, width:]
    high = inner.astype(BF16)
    sent_ref[:, pl.ds(width, inner.shape[1])] = high
    sent_ref[:, pl.ds(width + inner.shape[1], inner.shape[1])] = (
        inner - high.astype(F32)
    ).astype(BF16)
    for k, out in enumerate(outs):
        out[:, pl.ds(0, width)] = right
        out[:, pl.ds(width, share)] = rest[row ^ k].astype(BF16)


def route_kernel(peers, width, *refs):
    pieces, outs, inner_ref, held = refs[: -peers - 2], refs[-peers - 2 : -2], refs[-2], refs[-1]
    row, col = lax.axis_index("row"), lax.axis_index("col")
    count = len(pieces)
    per_block = count // peers
    measures = pieces[0].shape[0]
    overall = inner_ref.shape[0]
    total = jnp.zeros((measures, overall * peers), F32)
    for k, piece in enumerate(pieces):
        held[(col // 2) ^ k] = piece[:, pl.ds(0, width)]
        total = total + piece[:, pl.ds(width, overall * peers)].astype(F32)
        total = total + piece[:, pl.ds(width + overall * peers, overall * peers)].astype(F32)
    for q in range(peers):
        inner_ref[pl.ds(q * measures, measures), :] = total[:, q * overall : (q + 1) * overall]
    for k in range(peers):
        for p in range(per_block):
            outs[k][:, pl.ds(p * width, width)] = held[(row ^ k) * per_block + p]


def inverse_kernel(*refs):
    inner_refs, (noise_ref, innovation_ref, inverse_ref, weight_ref) = refs[:2], refs[2:]
    overall = inverse_ref.shape[0]
    inner = inner_refs[0][...] + inner_refs[1][...]
    down = lax.broadcasted_iota(jnp.int32, (overall, overall), 0)
    across = lax.broadcasted_iota(jnp.int32, (overall, overall), 1)
    diagonal = down == across
    inner = inner + jnp.where(diagonal, noise_ref[...], 0.0)
    scale = 1.0 / jnp.max(jnp.sum(jnp.abs(inner), axis=1, keepdims=True), axis=0, keepdims=True)
    inverse = jnp.where(diagonal, scale, 0.0)
    for _ in range(NS_ITERS):
        left = jnp.dot(inverse, inner, precision=FULL, preferred_element_type=F32)
        inverse = 2.0 * inverse - jnp.dot(left, inverse, precision=FULL, preferred_element_type=F32)
    inverse_ref[...] = inverse
    weight_ref[...] = jnp.sum(inverse * innovation_ref[...], axis=1, keepdims=True)


def merge_kernel(peers, weight_ref, *refs):
    pieces, blocks = refs[:peers], refs[peers : 2 * peers]
    half_ref, right_ref, change_ref = refs[2 * peers :]
    me = lax.axis_index("row")
    width = right_ref.shape[1]
    share = width // peers
    measures = pieces[0].shape[0]
    arrange(half_ref, pieces, 0, half_ref.shape[1])
    arrange(right_ref, blocks, 0, width)
    total = jnp.zeros((measures, share), F32)
    for k, block in enumerate(blocks):
        at = pl.multiple_of((me ^ k) * measures, measures)
        right = block[:, pl.ds(0, width)].astype(F32)
        exact = block[:, pl.ds(width, share)].astype(F32)
        for q in range(peers):
            exact = exact + jnp.where(me == q, right[:, q * share : (q + 1) * share], 0.0)
        total = total + weight_ref[pl.ds(at, measures), :] * exact
    change_ref[...] = jnp.sum(total, axis=0, keepdims=True)


def update_kernel(depth, weights_ref, moved_ref, *refs):
    mine_ref, other_ref, right_ref, inverse_ref = refs[:4]
    kept, (cov_ref, weights_new_ref, out_ref) = refs[4:-11], refs[-11:-8]
    numerator, left, fresh, done, loaded, sems, fixed, fixed_sem = refs[-8:]
    height, width = cov_ref.shape
    skipped = height - fresh.shape[0]
    size = kept[0].shape[0]
    copies = loads(
        cov_ref,
        skipped,
        [fresh.at[pl.ds(at, size), :] for at in range(0, height - skipped, size)],
        loaded,
    )
    for copy in copies:
        copy.start()
    fixed[...] = weights_ref[...] + moved_ref[0, :]
    fix = pltpu.make_async_copy(fixed, weights_new_ref, fixed_sem)
    fix.start()
    core = lax.axis_index("col") % 2
    for p in range(height // (2 * width)):
        part = pl.ds(p * width, width)
        here, there = mine_ref[:, part], other_ref[:, part]
        numerator[:, pl.ds(2 * p * width, width)] = jnp.where(core == 0, here, there)
        numerator[:, pl.ds((2 * p + 1) * width, width)] = jnp.where(core == 0, there, here)
    slots = done.shape[0]

    def leave(slot, at):
        return pltpu.make_async_copy(
            done.at[slot], out_ref.at[pl.ds(at, depth), :], sems.at[slot]
        )

    parts = [(part, 0, None) for part in kept]
    parts += [(fresh, k * size, copy) for k, copy in enumerate(copies)]
    for k, (part, base, copy) in enumerate(parts):
        left[...] = lax.dot_general(
            inverse_ref[...],
            numerator[:, pl.ds(k * size, size)].astype(F32),
            (((0,), (0,)), ((), ())),
            precision=FULL,
            preferred_element_type=F32,
        ).astype(BF16)
        if copy is not None:
            copy.wait()

        def tile(i, carry, k=k, part=part, base=base):
            at = pl.multiple_of(i * depth, depth)
            gain = left[:, pl.ds(at, depth)]
            count = i + k * (size // depth)
            slot = lax.rem(count, slots)

            @pl.when(count >= slots)
            def _():
                leave(slot, 0).wait()

            for start in range(0, width, CUT):
                cut = pl.ds(start, min(CUT, width - start))
                done[slot, :, cut] = part[pl.ds(base + at, depth), cut] - lax.dot_general(
                    gain, right_ref[:, cut], (((0,), (0,)), ((), ())), preferred_element_type=F32
                )
            leave(slot, pl.multiple_of(k * size + at, depth)).start()
            return carry

        lax.fori_loop(0, size // depth, tile, 0)
    for slot in range(slots):
        leave(slot, 0).wait()
    fix.wait()


def on_device(
    cov,
    weights,
    act,
    upstream,
    neighbors,
    types,
    type_gain,
    sens,
    frame_for_measure,
    noise_variance,
    innovation,
):
    rows, cols = lax.axis_size("row"), lax.axis_size("col")
    frames, atoms, width_in = act.shape
    width_out = upstream.shape[2]
    slots = neighbors.shape[2]
    lanes = frames * atoms
    measures = sens.shape[0]
    overall = measures * rows
    height, width = cov.shape
    part = weights.shape[0]
    dma = pltpu.SemaphoreType.DMA
    depth = next(d for d in (256, 128) if height % d == 0)
    tiles = height // depth
    each = next(n for n in EACH if tiles % n == 0)
    segments = tiles // each
    held = resident((each * depth, width))
    early, later = segments * EARLY // 6, segments * LATER // 6
    packed_width = width_out + -(-width_in // 128) * 128

    packed, near, kinds, scale, masked = pl.pallas_call(
        pack_kernel,
        out_shape=[
            shape((frames, atoms, packed_width), BF16),
            shape(neighbors.shape, jnp.int32),
            shape(types.shape, jnp.int32),
            shape(type_gain.shape),
            shape((measures, lanes)),
        ],
        in_specs=[ANY] * 7,
        out_specs=[VMEM] * 5,
        scratch_shapes=[
            pltpu.VMEM(upstream.shape, BF16),
            pltpu.VMEM(act.shape, BF16),
            pltpu.VMEM(sens.shape, F32),
            pltpu.SMEM(frame_for_measure.shape, jnp.int32),
            dma((7,)),
        ],
        compiler_params=params(3),
        name="pack",
    )(*map(outside, (upstream, act, neighbors, types, type_gain, sens, frame_for_measure)))
    packs = gather(packed)
    counts, *kept = pl.pallas_call(
        functools.partial(counts_kernel, 0),
        out_shape=[shape((atoms * cols, lanes), BF16)] + [held] * early,
        in_specs=[VMEM, ANY],
        out_specs=[VMEM] * (1 + early),
        scratch_shapes=[pltpu.VMEM((slots, lanes), jnp.int32), dma((early,))],
        compiler_params=params(3),
        cost_estimate=estimate(3 * 10**9, 4 * early * each * depth * width),
        name="counts",
    )(near, outside(cov))
    side = pl.pallas_call(
        functools.partial(adjoint_kernel, slots, width_out),
        out_shape=shape((width_out + measures, lanes)),
        in_specs=[VMEM] * (4 + cols),
        out_specs=VMEM,
        scratch_shapes=[pltpu.VMEM((frames, atoms * cols, width_out), BF16)],
        compiler_params=params(3),
        name="adjoint",
    )(counts, kinds, scale, masked, *packs)
    sides = gather(side)
    part_a = tiles // 2 // each * each * depth
    part_b = height - part_a
    kept = list(kept)
    jacs = []
    for skip, size, extra, loaded in (
        (0, part_a, 0, later // 2),
        (part_a, part_b, width, later - later // 2),
    ):
        found = pl.pallas_call(
            functools.partial(
                jacobian_kernel, cols, rows, width_in, skip, size, len(kept) * each * depth
            ),
            out_shape=[shape((measures, size + extra), BF16)] * rows + [held] * loaded,
            in_specs=[VMEM] * (2 * cols) + [ANY],
            out_specs=[VMEM] * (rows + loaded),
            scratch_shapes=[
                pltpu.VMEM((cols * lanes, width_in), BF16),
                pltpu.VMEM((8 * measures, cols * lanes), BF16),
                pltpu.VMEM((measures, 8 * width_in), F32),
                dma((max(1, loaded),)),
            ],
            compiler_params=params(5),
            cost_estimate=estimate(3 * 10**9, 4 * loaded * each * depth * width),
            name="jacobian_last" if skip else "jacobian_first",
        )(*sides, *packs, outside(cov))
        kept += found[rows:]
        jacs.append(exchange(found[:rows]))
    first = part_a // (each * depth)
    begun = pl.pallas_call(
        functools.partial(product_first_kernel, rows, depth),
        out_shape=shape((overall, width)),
        in_specs=[VMEM] * (rows + first),
        out_specs=VMEM,
        scratch_shapes=[pltpu.VMEM((overall, part_a), BF16)],
        compiler_params=params(9),
        cost_estimate=estimate(8 * overall * part_a * width, 4 * part_a * width),
        name="product_first",
    )(*jacs[0], *map(keep, kept[:first]))
    rest = len(kept) - first
    parts = pl.pallas_call(
        functools.partial(product_last_kernel, rows, depth, rest),
        out_shape=[shape((measures, width + overall * rows))] * rows,
        in_specs=[VMEM] * (rows + 1 + rest) + [ANY],
        out_specs=[VMEM] * rows,
        scratch_shapes=[
            pltpu.VMEM((overall, part_b), BF16),
            pltpu.VMEM((overall, width), BF16),
            pltpu.VMEM((overall, width), F32),
            pltpu.VMEM((2, depth, width), F32),
            dma((2,)),
        ],
        compiler_params=params(14),
        cost_estimate=estimate(8 * overall * part_b * width, 4 * part_b * width),
        name="product_last",
    )(*jacs[1], begun, *map(keep, kept[first:]), outside(cov))
    parts = exchange(parts)
    sent, *blocks = pl.pallas_call(
        functools.partial(sum_kernel, rows),
        out_shape=[shape((measures, width + 2 * overall * rows), BF16)]
        + [shape((measures, width + part), BF16)] * rows,
        in_specs=[VMEM] * rows,
        out_specs=[VMEM] * (rows + 1),
        scratch_shapes=[pltpu.VMEM((rows, measures, part), F32)],
        compiler_params=params(3),
        name="sum",
    )(*parts)
    sents = gather_apart(sent)
    blocks = exchange(blocks)
    span = height // 2
    *routed, inner = pl.pallas_call(
        functools.partial(route_kernel, rows, width),
        out_shape=[shape((measures, span), BF16)] * rows + [shape((overall, overall))],
        in_specs=[VMEM] * (cols // 2),
        out_specs=[VMEM] * (rows + 1),
        scratch_shapes=[pltpu.VMEM((cols // 2, measures, width), BF16)],
        compiler_params=params(3),
        name="route",
    )(*sents)
    routed = exchange(routed)
    shared = swap(inner, "col", 1)
    inverse, weight = pl.pallas_call(
        inverse_kernel,
        out_shape=[shape((overall, overall)), shape((overall, 1))],
        in_specs=[VMEM] * 4,
        out_specs=[VMEM] * 2,
        compiler_params=params(3),
        name="inverse",
    )(inner, shared, noise_variance[None, :], innovation[None, :])
    half, right, change = pl.pallas_call(
        functools.partial(merge_kernel, rows),
        out_shape=[
            shape((overall, span), BF16),
            shape((overall, width), BF16),
            shape((1, part)),
        ],
        in_specs=[VMEM] * (1 + 2 * rows),
        out_specs=[VMEM] * 3,
        compiler_params=params(3),
        name="merge",
    )(weight, *routed, *blocks)
    other = swap(half, "col", 1)
    pairs = [(r * cols + c, c * rows + r) for r in range(rows) for c in range(cols)]
    moved = lax.ppermute(change, ("row", "col"), pairs)
    size = each * depth
    fresh = height - len(kept) * size
    weights_new, cov_new = pl.pallas_call(
        functools.partial(update_kernel, THIN),
        out_shape=[shape((part,)), shape((height, width))],
        in_specs=[VMEM] * (6 + len(kept)) + [ANY],
        out_specs=[ANY, ANY],
        scratch_shapes=[
            pltpu.VMEM((overall, height), BF16),
            pltpu.VMEM((overall, size), BF16),
            pltpu.VMEM((fresh, width), F32),
            pltpu.VMEM((SLOTS, THIN, width), F32),
            dma((fresh // size,)),
            dma((SLOTS,)),
            pltpu.VMEM((part,), F32),
            dma,
        ],
        compiler_params=params(15),
        cost_estimate=estimate(2 * overall * height * width, 4 * height * width),
        name="update",
    )(weights, moved, half, other, right, inverse, *map(keep, kept), outside(cov))
    return (weights_new, cov_new)


def solution(mesh):
    return jax.shard_map(
        on_device,
        mesh=mesh,
        in_specs=(
            P("row", "col"),
            P(("row", "col")),
            P("row", "col", None),
            P("row", "col", None),
            P("row", "col", None),
            P("row", "col"),
            P(),
            P("row", "col"),
            P("row"),
            P(),
            P(),
        ),
        out_specs=(P(("row", "col")), P("row", "col")),
        check_vma=False,
    )
```
